32 devices in a mesh: subj: 2 (over x), ha: 8 (over z, y), dev: 2 (over core).
Axes of the slice: x: 2, y: 2, z: 4, core: 2. Of those that a mesh axis runs over, the one named last changes fastest.
Arguments:
- brain_image: float32 [64, 256, 768], P('subj', 'ha', 'dev'), parts along dimension 0, may hold values from -6 to 6
- adjoint_field: float32 [64, 256, 768], P('subj', 'ha', 'dev'), parts along dimension 0, may hold values from -6 to 6
- velocity_modes: float32 [6, 16, 32, 32], P('subj'), parts along dimension 0, may hold values from -4 to 4
Outputs:
- adjoint_end: float32 [64, 256, 768], P('subj', 'ha', 'dev'), parts along dimension 0
- image_end: float32 [64, 256, 768], P('subj', 'ha', 'dev'), parts along dimension 0
- velocity_next: float32 [6, 16, 32, 32], P('subj'), parts along dimension 0
The draws below stay inside these ranges and needn't reach their ends.
There are 2 independent parts, one for each index of `subj`. The reference program is written for one: setup_inputs(seed, part) draws one part's arguments, and reference() takes and returns one part's arrays. A program takes and returns all parts, laid end to end along the dimension named above; each array names one. Nothing has to cross between parts.
All inputs are finite; a program needn't handle non-finite values.
Results may differ from the reference program's by a relative error of at most 0.0003.
Values sent between devices are 32-bit elements; how exact they have to be, the bound alone decides.
A program may use at most 128 MiB of HBM per device.

```python
import math
import jax
import jax.numpy as jnp
from jax import lax

PLANES = 32
MX = 16
M = 32
STEPS = 4
NY = 256
NZ = 768


def levels(key, extent, pieces, least, largest):
    loudness, own = 1.0, jax.random.fold_in(key, 6)
    for dim, shards_of in pieces:
        heights = jnp.exp(jax.random.uniform(jax.random.fold_in(own, dim), (shards_of,), jnp.float32, least / len(pieces), largest / len(pieces)))
        loudness = loudness * jnp.repeat(heights, extent[dim] // shards_of).reshape([-1 if axis == dim else 1 for axis in range(len(extent))])
    return loudness


def noise(stream_key, shape, deviation, reach, pieces=(), held_as=jnp.bfloat16):
    result = deviation * jax.random.normal(stream_key, shape, jnp.float32)
    if pieces:
        result = result * levels(stream_key, shape, pieces, -0.22, 0.18)
    return jnp.clip(result, -reach, reach).astype(held_as)


def setup_inputs(seed: int = 0, part: int = 0) -> dict:
    arg_keys = jax.random.split(jax.random.key(seed), 4)
    part_splits = jax.random.split(jax.random.fold_in(arg_keys[3], part), 4)
    return {
        "brain_image": noise(part_splits[0], (PLANES, NY, NZ), 1.0, 6.0, ((1, 8), (2, 2)), jnp.float32),
        "adjoint_field": noise(part_splits[1], (PLANES, NY, NZ), 1.0, 6.0, ((1, 8), (2, 2)), jnp.float32),
        "velocity_modes": noise(part_splits[2], (3, MX, M, M), 0.7, 4.0, (), jnp.float32),
    }


PRECISE = lax.Precision.HIGHEST
STEP_SIZE = 4.0
STIFFNESS = 2.0

def fourier_table(positions, length, modes):
    column = jnp.arange(modes, dtype=jnp.int32)
    middle_mode = modes // 2
    wavenumber = jnp.where(column <= middle_mode, column, column - middle_mode)
    phase_index = positions[:, None] * wavenumber[None, :] % length
    angles = phase_index.astype(jnp.float32) * (2.0 * math.pi / length)
    return jnp.where(column[None, :] <= middle_mode, jnp.cos(angles), jnp.sin(angles))

def dimension_terms(length, modes):
    column = jnp.arange(modes, dtype=jnp.int32)
    middle_mode = modes // 2
    wavenumber = jnp.where(column <= middle_mode, column, column - middle_mode)
    eigenvalue = 2.0 - 2.0 * jnp.cos(wavenumber.astype(jnp.float32) * (2.0 * math.pi / length))
    weight = jnp.where(column == 0, jnp.float32(length), jnp.float32(length / 2.0))
    return (eigenvalue, weight)

def mode_factor(planes, height, depth, modes_x, modes_yz):
    eigen_x, weight_x = dimension_terms(planes, modes_x)
    eigen_y, weight_y = dimension_terms(height, modes_yz)
    eigen_z, weight_z = dimension_terms(depth, modes_yz)
    eigenvalue = eigen_x[:, None, None] + eigen_y[None, :, None] + eigen_z[None, None, :]
    squared_norm = weight_x[:, None, None] * weight_y[None, :, None] * weight_z[None, None, :]
    mode_count = modes_x * modes_yz * modes_yz
    factor = STEP_SIZE * math.sqrt(mode_count) / (squared_norm * jnp.square(1.0 + STIFFNESS * eigenvalue))
    return factor.reshape(-1)

def expand(coeffs, table_x, table_y, table_z):
    mode_count = coeffs.shape[1] * coeffs.shape[2] * coeffs.shape[3]
    scaled = coeffs * (1.0 / math.sqrt(mode_count))
    inner = jnp.einsum('cabk,xa->cxbk', scaled, table_x, precision=PRECISE)
    inner = jnp.einsum('cxbk,yb->cxyk', inner, table_y, precision=PRECISE)
    return jnp.einsum('cxyk,zk->cxyz', inner, table_z, precision=PRECISE)

def project(forcing, table_x, table_y, table_z):
    inner = jnp.einsum('cxyz,zk->cxyk', forcing, table_z, precision=PRECISE)
    inner = jnp.einsum('cxyk,yb->cxbk', inner, table_y, precision=PRECISE)
    return jnp.einsum('cxbk,xa->cabk', inner, table_x, precision=PRECISE)

def upwind_rate(padded, speed):
    center = padded[1:-1, 1:-1, 1:-1]
    behind = (center - padded[:-2, 1:-1, 1:-1], center - padded[1:-1, :-2, 1:-1], center - padded[1:-1, 1:-1, :-2])
    ahead = (padded[2:, 1:-1, 1:-1] - center, padded[1:-1, 2:, 1:-1] - center, padded[1:-1, 1:-1, 2:] - center)
    summed = jnp.zeros_like(center)
    for direction in range(3):
        summed = summed + jnp.maximum(speed[direction], 0.0) * behind[direction] + jnp.minimum(speed[direction], 0.0) * ahead[direction]
    return -summed

def central_gradient(padded):
    return jnp.stack([0.5 * (padded[2:, 1:-1, 1:-1] - padded[:-2, 1:-1, 1:-1]), 0.5 * (padded[1:-1, 2:, 1:-1] - padded[1:-1, :-2, 1:-1]), 0.5 * (padded[1:-1, 1:-1, 2:] - padded[1:-1, 1:-1, :-2])])

def advance(current, speed):
    middle = current + 1.0 * upwind_rate(jnp.pad(current, 1), speed)
    second = upwind_rate(jnp.pad(middle, 1), speed)
    return 0.5 * (current + middle + 1.0 * second)

def reference(brain_image, adjoint_field, velocity_modes):
    planes, height, depth = brain_image.shape
    modes_x = velocity_modes.shape[1]
    modes_yz = velocity_modes.shape[2]
    table_x = fourier_table(jnp.arange(planes, dtype=jnp.int32), planes, modes_x)
    table_y = fourier_table(jnp.arange(height, dtype=jnp.int32), height, modes_yz)
    table_z = fourier_table(jnp.arange(depth, dtype=jnp.int32), depth, modes_yz)
    old_speed = expand(velocity_modes, table_x, table_y, table_z)
    backward = -old_speed
    current = adjoint_field
    for repeat in range(STEPS):
        current = advance(current, backward)
    adjoint_end = current
    forcing = adjoint_end[None] * central_gradient(jnp.pad(brain_image, 1))
    partial_value = project(forcing, table_x, table_y, table_z).reshape(3, -1)
    factor = mode_factor(planes, height, depth, modes_x, modes_yz)
    flat_next = velocity_modes.reshape(3, -1) + factor[None, :] * partial_value
    velocity_next = flat_next.reshape(velocity_modes.shape)
    new_speed = expand(velocity_next, table_x, table_y, table_z)
    current = brain_image
    for repeat in range(STEPS):
        current = advance(current, new_speed)
    return (adjoint_end, current, velocity_next)
```

```python
import functools
import math

import jax
import jax.numpy as jnp
import ml_dtypes
import numpy as np
from jax import lax
from jax.experimental import pallas as pl
from jax.experimental.pallas import tpu as pltpu
from jax.sharding import PartitionSpec as P

STEPS = 4
HALO = 2 * STEPS
STEP_SIZE = 4.0
STIFFNESS = 2.0
LANES = 128
F32 = jnp.float32
BF16 = jnp.bfloat16


def wavenumbers(modes):
    column = np.arange(modes)
    return np.where(column <= modes // 2, column, column - modes // 2)


def basis(positions, length, modes):
    phase = positions[:, None] * wavenumbers(modes)[None, :] % length
    angles = phase * (2.0 * math.pi / length)
    cosine = np.arange(modes)[None, :] <= modes // 2
    table = np.where(cosine, np.cos(angles), np.sin(angles))
    inside = (positions >= 0) & (positions < length)
    return np.where(inside[:, None], table, 0.0).astype(np.float32)


def halves(table):
    high = table.astype(ml_dtypes.bfloat16)
    low = (table - high.astype(np.float32)).astype(ml_dtypes.bfloat16)
    return high, low


def wrapped(start, rows, total, length):
    gap = np.full(total - rows - 2 * HALO, -1)
    after = np.arange(start + rows, start + rows + HALO)
    before = np.arange(start - HALO, start)
    return np.concatenate([np.arange(start, start + rows), after, gap, before])


def mode_factor(lengths, modes):
    eigen, weight = [], []
    for length, count in zip(lengths, modes):
        eigen.append(2.0 - 2.0 * np.cos(wavenumbers(count) * (2.0 * math.pi / length)))
        weight.append(np.where(np.arange(count) == 0, length, length / 2.0))
    value = eigen[0][:, None, None] + eigen[1][None, :, None] + eigen[2][None, None, :]
    norm = weight[0][:, None, None] * weight[1][None, :, None] * weight[2][None, None, :]
    return STEP_SIZE * math.sqrt(math.prod(modes)) / (norm * (1.0 + STIFFNESS * value) ** 2)


def split(value):
    high = value.astype(BF16)
    return high, (value - high.astype(F32)).astype(BF16)


def expand_kernel(planes, modes_x, modes, v_ref, bx_ref, by_ref, bz_ref, coefs):
    height, depth = coefs[0].shape[1:]
    group = lax.broadcasted_iota(jnp.int32, (height, LANES), 1) // modes

    def body(x, carry):
        weighted = bx_ref[x, 0] * v_ref[0]
        for a in range(1, modes_x):
            weighted = weighted + bx_ref[x, a] * v_ref[a]
        high, low = split(weighted)
        rows = jnp.concatenate([high, low, high], axis=0)
        mixed = jnp.dot(by_ref[...], rows, preferred_element_type=F32)
        top = mixed.astype(BF16).astype(F32)
        rest = mixed - top
        total = jnp.ones((height, depth), F32)
        for c in range(3):
            first = pltpu.roll(top, (-c * modes) % LANES, 1) if c else top
            second = pltpu.roll(top, ((1 - c) * modes) % LANES, 1) if c != 1 else top
            third = pltpu.roll(rest, ((2 - c) * modes) % LANES, 1) if c != 2 else rest
            left = jnp.where(group == 0, first, jnp.where(group == 1, second, third))
            speed = jnp.dot(left.astype(BF16), bz_ref[...], preferred_element_type=F32)
            plus = jnp.maximum(speed, 0.0)
            minus = jnp.maximum(-speed, 0.0)
            coefs[1 + 2 * c][x] = plus
            coefs[2 + 2 * c][x] = minus
            total = total - (plus + minus)
        coefs[0][x] = total
        return carry

    lax.fori_loop(0, planes, body, 0)


def gather_field(q_ref, yh_ref, zt_ref, field):
    planes, rows, depth = q_ref.shape
    height = field.shape[1]
    field[0] = jnp.zeros(field.shape[1:], F32)
    field[planes + 1] = jnp.zeros(field.shape[1:], F32)

    def body(x, carry):
        field[x + 1, 0:rows, 0:depth] = q_ref[x]
        field[x + 1, rows:height, 0:depth] = yh_ref[x]
        field[x + 1, :, depth : depth + LANES] = zt_ref[x]
        return carry

    lax.fori_loop(0, planes, body, 0)


def stencil(src, x, coefs, rows, depth):
    height, width = src.shape[1:]
    strips = height // 8
    wanted = rows // 8
    row = lax.broadcasted_iota(jnp.int32, (8, depth), 0)
    tiles = {}
    ups = {}
    downs = {}

    def tile(t):
        t = t % strips
        if t not in tiles:
            tiles[t] = src[x + 1, 8 * t : 8 * t + 8, :]
        return tiles[t]

    def up(t):
        t = t % strips
        if t not in ups:
            ups[t] = pltpu.roll(tile(t)[:, :depth], 1, 0)
        return ups[t]

    def down(t):
        t = t % strips
        if t not in downs:
            downs[t] = pltpu.roll(tile(t)[:, :depth], 7, 0)
        return downs[t]

    results = []
    for t in range(wanted):
        part = pl.ds(8 * t, 8)

        def coef(index):
            return coefs[index][x, part, 0:depth]

        q = tile(t)
        total = coef(0) * q[:, :depth]
        total = total + coef(1) * src[x, part, 0:depth] + coef(2) * src[x + 2, part, 0:depth]
        total = total + coef(3) * jnp.where(row == 0, up(t - 1), up(t))
        total = total + coef(4) * jnp.where(row == 7, down(t + 1), down(t))
        total = total + coef(5) * pltpu.roll(q, 1, 1)[:, :depth]
        total = total + coef(6) * pltpu.roll(q, width - 1, 1)[:, :depth]
        results.append(total)
    return results


def transport_kernel(
    planes, modes_x, modes, v_ref, bx_ref, by_ref, bz_ref, q_ref, yh_ref, zt_ref, out_ref, *scratch
):
    field, middle = scratch[:2]
    coefs = scratch[2:]
    height, width = field.shape[1:]
    rows, depth = q_ref.shape[1:]
    gather_field(q_ref, yh_ref, zt_ref, field)
    middle[0] = jnp.zeros((height, width), F32)
    middle[planes + 1] = jnp.zeros((height, width), F32)
    expand_kernel(planes, modes_x, modes, v_ref, bx_ref, by_ref, bz_ref, coefs)

    def first(x, carry):
        for t, value in enumerate(stencil(field, x, coefs, height, width)):
            middle[x + 1, 8 * t : 8 * t + 8, :] = value
        return carry

    def second(x, carry):
        for t, value in enumerate(stencil(middle, x, coefs, height, width)):
            part = pl.ds(8 * t, 8)
            field[x + 1, part, :] = 0.5 * (field[x + 1, part, :] + value)
        return carry

    def last(x, carry):
        for t, value in enumerate(stencil(middle, x, coefs, rows, depth)):
            part = pl.ds(8 * t, 8)
            out_ref[x, part, :] = 0.5 * (field[x + 1, part, 0:depth] + value)
        return carry

    def step(i, carry):
        lax.fori_loop(0, planes, first, 0)
        lax.fori_loop(0, planes, second, 0)
        return carry

    lax.fori_loop(0, STEPS - 1, step, 0)
    lax.fori_loop(0, planes, first, 0)
    lax.fori_loop(0, planes, last, 0)


def project_kernel(
    planes, modes_x, adj_ref, q_ref, yh_ref, zt_ref, bx_ref, by_ref, bz_ref, out_ref, field, forcing, inner
):
    height, width = field.shape[1:]
    rows, depth = q_ref.shape[1:]
    gather_field(q_ref, yh_ref, zt_ref, field)

    def body(x, carry):
        plane = field[x + 1]
        half = 0.5 * adj_ref[x]
        slopes = (
            field[x + 2, 0:rows, 0:depth] - field[x, 0:rows, 0:depth],
            (pltpu.roll(plane, height - 1, 0) - pltpu.roll(plane, 1, 0))[0:rows, 0:depth],
            (pltpu.roll(plane, width - 1, 1) - pltpu.roll(plane, 1, 1))[0:rows, 0:depth],
        )
        for c in range(3):
            high, low = split(half * slopes[c])
            columns = slice(c * depth, (c + 1) * depth)
            forcing[pl.ds(x * 2 * rows, rows), columns] = high
            forcing[pl.ds(x * 2 * rows + rows, rows), columns] = low
        return carry

    lax.fori_loop(0, planes, body, 0)
    chunk = 8

    def multiply(i, carry):
        start = i * (chunk * 2 * rows)
        wide = jnp.dot(
            forcing[pl.ds(start, chunk * 2 * rows), :], bz_ref[...], preferred_element_type=F32
        )
        wide = wide[:, 0:LANES] + wide[:, LANES : 2 * LANES]
        wide = wide.reshape(chunk, 2 * rows, LANES)
        inner[pl.ds(i * chunk, chunk)] = wide[:, 0:rows] + wide[:, rows : 2 * rows]
        return carry

    lax.fori_loop(0, planes // chunk, multiply, 0)

    def finish(a, carry):
        total = bx_ref[0, a] * inner[0]
        for x in range(1, planes):
            total = total + bx_ref[x, a] * inner[x]
        high, low = split(total)
        stacked = jnp.concatenate([high, low, high], axis=0)
        out_ref[a] = jnp.dot(by_ref[...], stacked, preferred_element_type=F32)
        return carry

    lax.fori_loop(0, modes_x, finish, 0)


VMEM = pl.BlockSpec(memory_space=pltpu.VMEM)
SMEM = pl.BlockSpec(memory_space=pltpu.SMEM)
PARAMS = pltpu.CompilerParams(vmem_limit_bytes=60 * 1024 * 1024)


def halo_of(field):
    count = lax.axis_size("ha")
    forward = [(i, i + 1) for i in range(count - 1)]
    backward = [(i + 1, i) for i in range(count - 1)]
    before = lax.ppermute(field[:, -HALO:, :], "ha", forward)
    after = lax.ppermute(field[:, :HALO, :], "ha", backward)
    sides = lax.axis_size("dev")
    forward = [(i, i + 1) for i in range(sides - 1)]
    backward = [(i + 1, i) for i in range(sides - 1)]
    rows = jnp.concatenate([after, before], axis=1)
    head = jnp.concatenate([field[:, :, :HALO], rows[:, :, :HALO]], axis=1)
    tail = jnp.concatenate([field[:, :, -HALO:], rows[:, :, -HALO:]], axis=1)
    left = lax.ppermute(tail, "dev", forward)
    right = lax.ppermute(head, "dev", backward)
    gap = jnp.zeros(left.shape[:2] + (LANES - 2 * HALO,), F32)
    return rows, jnp.concatenate([right, gap, left], axis=2)


def per_device(brain_image, adjoint_field, velocity_modes):
    planes, rows, cols = brain_image.shape
    count_y = lax.axis_size("ha")
    count_z = lax.axis_size("dev")
    height, depth = rows * count_y, cols * count_z
    modes_x, modes = velocity_modes.shape[1:3]
    tall, wide = rows + 2 * HALO, cols + LANES
    index_y, index_z = lax.axis_index("ha"), lax.axis_index("dev")

    expand_y, expand_z, project_y, project_z = [], [], [], []
    for i in range(count_y):
        high, low = halves(basis(wrapped(i * rows, rows, tall, height), height, modes))
        expand_y.append(np.concatenate([high, high, low], axis=1))
        high, low = high[:rows].T, low[:rows].T
        project_y.append(np.concatenate([high, high, low], axis=1))
    for i in range(count_z):
        high, low = halves(basis(wrapped(i * cols, cols, wide, depth), depth, modes))
        high, low = high.T, low.T
        table = np.zeros((LANES, wide), ml_dtypes.bfloat16)
        table[: 3 * modes] = np.concatenate([high, low, high], axis=0)
        expand_z.append(table)
        table = np.zeros((3, cols, 2, LANES), ml_dtypes.bfloat16)
        for c in range(3):
            table[c, :, 0, c * modes : (c + 1) * modes] = high.T[:cols]
            table[c, :, 1, c * modes : (c + 1) * modes] = low.T[:cols]
        project_z.append(table.reshape(3 * cols, 2 * LANES))

    def pick(tables, index):
        return lax.dynamic_index_in_dim(jnp.asarray(np.stack(tables)), index, 0, keepdims=False)

    by_wide, by_back = pick(expand_y, index_y), pick(project_y, index_y)
    bz_wide, bz_back = pick(expand_z, index_z), pick(project_z, index_z)
    bx = jnp.asarray(basis(np.arange(planes), planes, modes_x))
    factor = mode_factor((planes, height, depth), (modes_x, modes, modes))
    factor = np.tile(factor, (1, 1, 3)).astype(np.float32)
    scale = 1.0 / math.sqrt(modes_x * modes * modes)

    def widen(value):
        return jnp.pad(value, ((0, 0), (0, 0), (0, LANES - 3 * modes)))

    plane = pltpu.VMEM((planes + 2, tall, wide), F32)
    transport = pl.pallas_call(
        functools.partial(transport_kernel, planes, modes_x, modes),
        out_shape=jax.ShapeDtypeStruct((planes, rows, cols), F32),
        in_specs=[VMEM, SMEM, VMEM, VMEM, VMEM, VMEM, VMEM],
        out_specs=VMEM,
        scratch_shapes=[plane, plane] + [pltpu.VMEM((planes, tall, wide), F32)] * 7,
        compiler_params=PARAMS,
        cost_estimate=pl.CostEstimate(
            flops=200 * planes * tall * wide, bytes_accessed=60_000_000, transcendentals=0
        ),
        name="transport",
    )
    project = pl.pallas_call(
        functools.partial(project_kernel, planes, modes_x),
        out_shape=jax.ShapeDtypeStruct((modes_x, modes, LANES), F32),
        in_specs=[VMEM, VMEM, VMEM, VMEM, SMEM, VMEM, VMEM],
        out_specs=VMEM,
        scratch_shapes=[
            plane,
            pltpu.VMEM((planes * 2 * rows, 3 * cols), BF16),
            pltpu.VMEM((planes, rows, LANES), F32),
        ],
        compiler_params=PARAMS,
        name="project",
    )

    old = velocity_modes.transpose(1, 2, 0, 3).reshape(modes_x, modes, 3 * modes)
    adjoint_halo = halo_of(adjoint_field)
    image_halo = halo_of(brain_image)
    adjoint_end = transport(
        widen(old * -scale), bx, by_wide, bz_wide, adjoint_field, *adjoint_halo
    )
    partial = project(adjoint_end, brain_image, *image_halo, bx, by_back, bz_back)
    summed = lax.psum(partial[:, :, : 3 * modes], ("ha", "dev"))
    updated = old + factor * summed
    image_end = transport(widen(updated * scale), bx, by_wide, bz_wide, brain_image, *image_halo)
    velocity_next = updated.reshape(modes_x, modes, 3, modes).transpose(2, 0, 1, 3)
    return (adjoint_end, image_end, velocity_next)


def solution(mesh):
    placed = (P("subj", "ha", "dev"), P("subj", "ha", "dev"), P("subj", None, None, None))
    return jax.shard_map(
        per_device,
        mesh=mesh,
        in_specs=placed,
        out_specs=placed,
        check_vma=False,
    )
```

```python
import functools
import math

import jax
import jax.numpy as jnp
import ml_dtypes
import numpy as np
from jax import lax
from jax.experimental import pallas as pl
from jax.experimental.pallas import tpu as pltpu
from jax.sharding import PartitionSpec as P

STEPS = 4
HALO = 2 * STEPS
STEP_SIZE = 4.0
STIFFNESS = 2.0
LANES = 128
F32 = jnp.float32
BF16 = jnp.bfloat16


def wavenumbers(modes):
    column = np.arange(modes)
    return np.where(column <= modes // 2, column, column - modes // 2)


def basis(positions, length, modes):
    phase = positions[:, None] * wavenumbers(modes)[None, :] % length
    angles = phase * (2.0 * math.pi / length)
    cosine = np.arange(modes)[None, :] <= modes // 2
    table = np.where(cosine, np.cos(angles), np.sin(angles))
    inside = (positions >= 0) & (positions < length)
    return np.where(inside[:, None], table, 0.0).astype(np.float32)


def halves(table):
    high = table.astype(ml_dtypes.bfloat16)
    low = (table - high.astype(np.float32)).astype(ml_dtypes.bfloat16)
    return high, low


def wrapped(start, rows, total, length):
    gap = np.full(total - rows - 2 * HALO, -1)
    after = np.arange(start + rows, start + rows + HALO)
    before = np.arange(start - HALO, start)
    return np.concatenate([np.arange(start, start + rows), after, gap, before])


def mode_factor(lengths, modes):
    eigen, weight = [], []
    for length, count in zip(lengths, modes):
        eigen.append(2.0 - 2.0 * np.cos(wavenumbers(count) * (2.0 * math.pi / length)))
        weight.append(np.where(np.arange(count) == 0, length, length / 2.0))
    value = eigen[0][:, None, None] + eigen[1][None, :, None] + eigen[2][None, None, :]
    norm = weight[0][:, None, None] * weight[1][None, :, None] * weight[2][None, None, :]
    return STEP_SIZE * math.sqrt(math.prod(modes)) / (norm * (1.0 + STIFFNESS * value) ** 2)


def split(value):
    high = value.astype(BF16)
    return high, (value - high.astype(F32)).astype(BF16)


def expand_kernel(planes, modes_x, modes, v_ref, bx_ref, by_ref, bz_ref, coefs):
    height, depth = coefs[0].shape[1:]
    group = lax.broadcasted_iota(jnp.int32, (height, LANES), 1) // modes

    def body(x, carry):
        weighted = bx_ref[x, 0] * v_ref[0]
        for a in range(1, modes_x):
            weighted = weighted + bx_ref[x, a] * v_ref[a]
        high, low = split(weighted)
        rows = jnp.concatenate([high, low, high], axis=0)
        mixed = jnp.dot(by_ref[...], rows, preferred_element_type=F32)
        top = mixed.astype(BF16).astype(F32)
        rest = mixed - top
        total = jnp.ones((height, depth), F32)
        for c in range(3):
            first = pltpu.roll(top, (-c * modes) % LANES, 1) if c else top
            second = pltpu.roll(top, ((1 - c) * modes) % LANES, 1) if c != 1 else top
            third = pltpu.roll(rest, ((2 - c) * modes) % LANES, 1) if c != 2 else rest
            left = jnp.where(group == 0, first, jnp.where(group == 1, second, third))
            speed = jnp.dot(left.astype(BF16), bz_ref[...], preferred_element_type=F32)
            plus = jnp.maximum(speed, 0.0)
            minus = jnp.maximum(-speed, 0.0)
            coefs[1 + 2 * c][x] = plus
            coefs[2 + 2 * c][x] = minus
            total = total - (plus + minus)
        coefs[0][x] = total
        return carry

    lax.fori_loop(0, planes, body, 0)


def gather_field(q_ref, yh_ref, zt_ref, field):
    planes, rows, depth = q_ref.shape
    height = field.shape[1]
    field[0] = jnp.zeros(field.shape[1:], F32)
    field[planes + 1] = jnp.zeros(field.shape[1:], F32)

    def body(x, carry):
        field[x + 1, 0:rows, 0:depth] = q_ref[x]
        field[x + 1, rows:height, 0:depth] = yh_ref[x]
        field[x + 1, :, depth : depth + LANES] = zt_ref[x]
        return carry

    lax.fori_loop(0, planes, body, 0)


def stencil(src, x, coefs, rows, depth):
    height, width = src.shape[1:]
    strips = height // 8
    wanted = rows // 8
    row = lax.broadcasted_iota(jnp.int32, (8, depth), 0)
    tiles = {}
    ups = {}
    downs = {}

    def tile(t):
        t = t % strips
        if t not in tiles:
            tiles[t] = src[x + 1, 8 * t : 8 * t + 8, :]
        return tiles[t]

    def up(t):
        t = t % strips
        if t not in ups:
            ups[t] = pltpu.roll(tile(t)[:, :depth], 1, 0)
        return ups[t]

    def down(t):
        t = t % strips
        if t not in downs:
            downs[t] = pltpu.roll(tile(t)[:, :depth], 7, 0)
        return downs[t]

    results = []
    for t in range(wanted):
        part = pl.ds(8 * t, 8)

        def coef(index):
            return coefs[index][x, part, 0:depth]

        q = tile(t)
        total = coef(0) * q[:, :depth]
        total = total + coef(1) * src[x, part, 0:depth] + coef(2) * src[x + 2, part, 0:depth]
        total = total + coef(3) * jnp.where(row == 0, up(t - 1), up(t))
        total = total + coef(4) * jnp.where(row == 7, down(t + 1), down(t))
        total = total + coef(5) * pltpu.roll(q, 1, 1)[:, :depth]
        total = total + coef(6) * pltpu.roll(q, width - 1, 1)[:, :depth]
        results.append(total)
    return results


def transport_kernel(
    planes, modes_x, modes, v_ref, bx_ref, by_ref, bz_ref, q_ref, yh_ref, zt_ref, out_ref, *scratch
):
    field, middle = scratch[:2]
    coefs = scratch[2:]
    height, width = field.shape[1:]
    rows, depth = q_ref.shape[1:]
    gather_field(q_ref, yh_ref, zt_ref, field)
    middle[0] = jnp.zeros((height, width), F32)
    middle[planes + 1] = jnp.zeros((height, width), F32)
    expand_kernel(planes, modes_x, modes, v_ref, bx_ref, by_ref, bz_ref, coefs)

    def first(x, carry):
        for t, value in enumerate(stencil(field, x, coefs, height, width)):
            middle[x + 1, 8 * t : 8 * t + 8, :] = value
        return carry

    def second(x, carry):
        for t, value in enumerate(stencil(middle, x, coefs, height, width)):
            part = pl.ds(8 * t, 8)
            field[x + 1, part, :] = 0.5 * (field[x + 1, part, :] + value)
        return carry

    def last(x, carry):
        for t, value in enumerate(stencil(middle, x, coefs, rows, depth)):
            part = pl.ds(8 * t, 8)
            out_ref[x, part, :] = 0.5 * (field[x + 1, part, 0:depth] + value)
        return carry

    def step(i, carry):
        lax.fori_loop(0, planes, first, 0)
        lax.fori_loop(0, planes, second, 0)
        return carry

    lax.fori_loop(0, STEPS - 1, step, 0)
    lax.fori_loop(0, planes, first, 0)
    lax.fori_loop(0, planes, last, 0)


def project_kernel(
    planes, modes_x, adj_ref, q_ref, yh_ref, zt_ref, bx_ref, by_ref, bz_ref, out_ref, field, forcing, inner
):
    height, width = field.shape[1:]
    rows, depth = q_ref.shape[1:]
    gather_field(q_ref, yh_ref, zt_ref, field)

    def body(x, carry):
        plane = field[x + 1]
        half = 0.5 * adj_ref[x]
        slopes = (
            field[x + 2, 0:rows, 0:depth] - field[x, 0:rows, 0:depth],
            (pltpu.roll(plane, height - 1, 0) - pltpu.roll(plane, 1, 0))[0:rows, 0:depth],
            (pltpu.roll(plane, width - 1, 1) - pltpu.roll(plane, 1, 1))[0:rows, 0:depth],
        )
        for c in range(3):
            high, low = split(half * slopes[c])
            columns = slice(c * depth, (c + 1) * depth)
            forcing[pl.ds(x * 2 * rows, rows), columns] = high
            forcing[pl.ds(x * 2 * rows + rows, rows), columns] = low
        return carry

    lax.fori_loop(0, planes, body, 0)
    chunk = 8

    def multiply(i, carry):
        start = i * (chunk * 2 * rows)
        wide = jnp.dot(
            forcing[pl.ds(start, chunk * 2 * rows), :], bz_ref[...], preferred_element_type=F32
        )
        wide = wide[:, 0:LANES] + wide[:, LANES : 2 * LANES]
        wide = wide.reshape(chunk, 2 * rows, LANES)
        inner[pl.ds(i * chunk, chunk)] = wide[:, 0:rows] + wide[:, rows : 2 * rows]
        return carry

    lax.fori_loop(0, planes // chunk, multiply, 0)

    def finish(a, carry):
        total = bx_ref[0, a] * inner[0]
        for x in range(1, planes):
            total = total + bx_ref[x, a] * inner[x]
        high, low = split(total)
        stacked = jnp.concatenate([high, low, high], axis=0)
        out_ref[a] = jnp.dot(by_ref[...], stacked, preferred_element_type=F32)
        return carry

    lax.fori_loop(0, modes_x, finish, 0)


def peer_of(index, sides):
    return {"ha": index // sides, "dev": lax.rem(index, sides)}


def update_kernel(count, sides, part_ref, old_ref, factor_ref, out_ref, held, send, recv, send2, recv2):
    me = lax.axis_index("ha") * sides + lax.axis_index("dev")
    rows = held.shape[1]
    barrier = pltpu.get_barrier_semaphore()
    for d in range(1, count):
        peer = lax.rem(me + d, count)
        pl.semaphore_signal(
            barrier, inc=1, device_id=peer_of(peer, sides), device_id_type=pl.DeviceIdType.MESH
        )
    pl.semaphore_wait(barrier, count - 1)
    mine = pl.ds(pl.multiple_of(me * rows, rows), rows)
    copies = []
    for d in range(1, count):
        peer = lax.rem(me + d, count)
        copy = pltpu.make_async_remote_copy(
            src_ref=part_ref.at[pl.ds(pl.multiple_of(peer * rows, rows), rows)],
            dst_ref=held.at[d],
            send_sem=send.at[d],
            recv_sem=recv.at[d],
            device_id=peer_of(peer, sides),
            device_id_type=pl.DeviceIdType.MESH,
        )
        copy.start()
        copies.append(copy)
    total = part_ref[mine]
    for d in range(1, count):
        copies[d - 1].wait_recv()
        total = total + held[d]
    out_ref[mine] = old_ref[mine] + factor_ref[mine] * total
    for copy in copies:
        copy.wait_send()
    copies = []
    for d in range(1, count):
        peer = lax.rem(me + d, count)
        copy = pltpu.make_async_remote_copy(
            src_ref=out_ref.at[mine],
            dst_ref=out_ref.at[mine],
            send_sem=send2.at[d],
            recv_sem=recv2.at[d],
            device_id=peer_of(peer, sides),
            device_id_type=pl.DeviceIdType.MESH,
        )
        copy.start()
        copies.append(copy)
    for copy in copies:
        copy.wait()


VMEM = pl.BlockSpec(memory_space=pltpu.VMEM)
SMEM = pl.BlockSpec(memory_space=pltpu.SMEM)
PARAMS = pltpu.CompilerParams(vmem_limit_bytes=60 * 1024 * 1024)


def halo_of(field):
    count = lax.axis_size("ha")
    forward = [(i, i + 1) for i in range(count - 1)]
    backward = [(i + 1, i) for i in range(count - 1)]
    before = lax.ppermute(field[:, -HALO:, :], "ha", forward)
    after = lax.ppermute(field[:, :HALO, :], "ha", backward)
    sides = lax.axis_size("dev")
    forward = [(i, i + 1) for i in range(sides - 1)]
    backward = [(i + 1, i) for i in range(sides - 1)]
    rows = jnp.concatenate([after, before], axis=1)
    head = jnp.concatenate([field[:, :, :HALO], rows[:, :, :HALO]], axis=1)
    tail = jnp.concatenate([field[:, :, -HALO:], rows[:, :, -HALO:]], axis=1)
    left = lax.ppermute(tail, "dev", forward)
    right = lax.ppermute(head, "dev", backward)
    gap = jnp.zeros(left.shape[:2] + (LANES - 2 * HALO,), F32)
    return rows, jnp.concatenate([right, gap, left], axis=2)


def per_device(brain_image, adjoint_field, velocity_modes):
    planes, rows, cols = brain_image.shape
    count_y = lax.axis_size("ha")
    count_z = lax.axis_size("dev")
    height, depth = rows * count_y, cols * count_z
    modes_x, modes = velocity_modes.shape[1:3]
    tall, wide = rows + 2 * HALO, cols + LANES
    index_y, index_z = lax.axis_index("ha"), lax.axis_index("dev")

    expand_y, expand_z, project_y, project_z = [], [], [], []
    for i in range(count_y):
        high, low = halves(basis(wrapped(i * rows, rows, tall, height), height, modes))
        expand_y.append(np.concatenate([high, high, low], axis=1))
        high, low = high[:rows].T, low[:rows].T
        project_y.append(np.concatenate([high, high, low], axis=1))
    for i in range(count_z):
        high, low = halves(basis(wrapped(i * cols, cols, wide, depth), depth, modes))
        high, low = high.T, low.T
        table = np.zeros((LANES, wide), ml_dtypes.bfloat16)
        table[: 3 * modes] = np.concatenate([high, low, high], axis=0)
        expand_z.append(table)
        table = np.zeros((3, cols, 2, LANES), ml_dtypes.bfloat16)
        for c in range(3):
            table[c, :, 0, c * modes : (c + 1) * modes] = high.T[:cols]
            table[c, :, 1, c * modes : (c + 1) * modes] = low.T[:cols]
        project_z.append(table.reshape(3 * cols, 2 * LANES))

    def pick(tables, index):
        return lax.dynamic_index_in_dim(jnp.asarray(np.stack(tables)), index, 0, keepdims=False)

    by_wide, by_back = pick(expand_y, index_y), pick(project_y, index_y)
    bz_wide, bz_back = pick(expand_z, index_z), pick(project_z, index_z)
    bx = jnp.asarray(basis(np.arange(planes), planes, modes_x))
    factor = mode_factor((planes, height, depth), (modes_x, modes, modes))
    factor = np.tile(factor, (1, 1, LANES // modes)).astype(np.float32).reshape(-1, LANES)
    scale = 1.0 / math.sqrt(modes_x * modes * modes)

    def widen(value):
        return jnp.pad(value, ((0, 0), (0, 0), (0, LANES - 3 * modes)))

    plane = pltpu.VMEM((planes + 2, tall, wide), F32)
    transport = pl.pallas_call(
        functools.partial(transport_kernel, planes, modes_x, modes),
        out_shape=jax.ShapeDtypeStruct((planes, rows, cols), F32),
        in_specs=[VMEM, SMEM, VMEM, VMEM, VMEM, VMEM, VMEM],
        out_specs=VMEM,
        scratch_shapes=[plane, plane] + [pltpu.VMEM((planes, tall, wide), F32)] * 7,
        compiler_params=PARAMS,
        cost_estimate=pl.CostEstimate(
            flops=200 * planes * tall * wide, bytes_accessed=60_000_000, transcendentals=0
        ),
        name="transport",
    )
    project = pl.pallas_call(
        functools.partial(project_kernel, planes, modes_x),
        out_shape=jax.ShapeDtypeStruct((modes_x, modes, LANES), F32),
        in_specs=[VMEM, VMEM, VMEM, VMEM, SMEM, VMEM, VMEM],
        out_specs=VMEM,
        scratch_shapes=[
            plane,
            pltpu.VMEM((planes * 2 * rows, 3 * cols), BF16),
            pltpu.VMEM((planes, rows, LANES), F32),
        ],
        compiler_params=PARAMS,
        name="project",
    )

    devices = count_y * count_z
    entries = modes_x * modes
    update = pl.pallas_call(
        functools.partial(update_kernel, devices, count_z),
        out_shape=jax.ShapeDtypeStruct((entries, LANES), F32),
        in_specs=[VMEM, VMEM, VMEM],
        out_specs=VMEM,
        scratch_shapes=[pltpu.VMEM((devices, entries // devices, LANES), F32)]
        + [pltpu.SemaphoreType.DMA((devices,))] * 4,
        compiler_params=pltpu.CompilerParams(collective_id=0, has_side_effects=True),
        name="update",
    )

    old = widen(velocity_modes.transpose(1, 2, 0, 3).reshape(modes_x, modes, 3 * modes))
    adjoint_halo = halo_of(adjoint_field)
    image_halo = halo_of(brain_image)
    adjoint_end = transport(old, bx * -scale, by_wide, bz_wide, adjoint_field, *adjoint_halo)
    partial = project(adjoint_end, brain_image, *image_halo, bx, by_back, bz_back)
    updated = update(partial.reshape(entries, LANES), old.reshape(entries, LANES), factor)
    updated = updated.reshape(modes_x, modes, LANES)
    image_end = transport(updated, bx * scale, by_wide, bz_wide, brain_image, *image_halo)
    velocity_next = updated[:, :, : 3 * modes].reshape(modes_x, modes, 3, modes)
    velocity_next = velocity_next.transpose(2, 0, 1, 3)
    return (adjoint_end, image_end, velocity_next)


def solution(mesh):
    placed = (P("subj", "ha", "dev"), P("subj", "ha", "dev"), P("subj", None, None, None))
    return jax.shard_map(
        per_device,
        mesh=mesh,
        in_specs=placed,
        out_specs=placed,
        check_vma=False,
    )
```

```python
import functools
import math

import jax
import jax.numpy as jnp
import ml_dtypes
import numpy as np
from jax import lax
from jax.experimental import pallas as pl
from jax.experimental.pallas import tpu as pltpu
from jax.sharding import PartitionSpec as P

STEPS = 4
HALO = 2 * STEPS
STEP_SIZE = 4.0
STIFFNESS = 2.0
LANES = 128
F32 = jnp.float32
BF16 = jnp.bfloat16


def wavenumbers(modes):
    column = np.arange(modes)
    return np.where(column <= modes // 2, column, column - modes // 2)


def basis(positions, length, modes):
    phase = positions[:, None] * wavenumbers(modes)[None, :] % length
    angles = phase * (2.0 * math.pi / length)
    cosine = np.arange(modes)[None, :] <= modes // 2
    table = np.where(cosine, np.cos(angles), np.sin(angles))
    inside = (positions >= 0) & (positions < length)
    return np.where(inside[:, None], table, 0.0).astype(np.float32)


def halves(table):
    high = table.astype(ml_dtypes.bfloat16)
    low = (table - high.astype(np.float32)).astype(ml_dtypes.bfloat16)
    return high, low


def wrapped(start, rows, total, length):
    gap = np.full(total - rows - 2 * HALO, -1)
    after = np.arange(start + rows, start + rows + HALO)
    before = np.arange(start - HALO, start)
    return np.concatenate([np.arange(start, start + rows), after, gap, before])


def mode_factor(lengths, modes):
    eigen, weight = [], []
    for length, count in zip(lengths, modes):
        eigen.append(2.0 - 2.0 * np.cos(wavenumbers(count) * (2.0 * math.pi / length)))
        weight.append(np.where(np.arange(count) == 0, length, length / 2.0))
    value = eigen[0][:, None, None] + eigen[1][None, :, None] + eigen[2][None, None, :]
    norm = weight[0][:, None, None] * weight[1][None, :, None] * weight[2][None, None, :]
    return STEP_SIZE * math.sqrt(math.prod(modes)) / (norm * (1.0 + STIFFNESS * value) ** 2)


def split(value):
    high = value.astype(BF16)
    return high, (value - high.astype(F32)).astype(BF16)


def expand_kernel(planes, modes_x, modes, v_ref, bx_ref, by_ref, bz_ref, coefs):
    height, depth = coefs[0].shape[1:]
    by, bz = by_ref[lax.axis_index("ha")], bz_ref.at[lax.axis_index("dev")]
    group = lax.broadcasted_iota(jnp.int32, (height, LANES), 1) // modes

    def body(x, carry):
        weighted = bx_ref[x, 0] * v_ref[0]
        for a in range(1, modes_x):
            weighted = weighted + bx_ref[x, a] * v_ref[a]
        high, low = split(weighted)
        rows = jnp.concatenate([high, low, high], axis=0)
        mixed = jnp.dot(by, rows, preferred_element_type=F32)
        top = mixed.astype(BF16).astype(F32)
        rest = mixed - top
        total = jnp.ones((height, depth), F32)
        for c in range(3):
            first = pltpu.roll(top, (-c * modes) % LANES, 1) if c else top
            second = pltpu.roll(top, ((1 - c) * modes) % LANES, 1) if c != 1 else top
            third = pltpu.roll(rest, ((2 - c) * modes) % LANES, 1) if c != 2 else rest
            left = jnp.where(group == 0, first, jnp.where(group == 1, second, third))
            speed = jnp.dot(left.astype(BF16), bz[...], preferred_element_type=F32)
            plus = jnp.maximum(speed, 0.0)
            minus = jnp.maximum(-speed, 0.0)
            coefs[1 + 2 * c][x] = plus
            coefs[2 + 2 * c][x] = minus
            total = total - (plus + minus)
        coefs[0][x] = total
        return carry

    lax.fori_loop(0, planes, body, 0, unroll=2)


def gather_field(q_ref, yh_ref, zt_ref, field):
    planes, rows, depth = q_ref.shape
    height = field.shape[1]
    field[0] = jnp.zeros(field.shape[1:], F32)
    field[planes + 1] = jnp.zeros(field.shape[1:], F32)

    def body(x, carry):
        field[x + 1, 0:rows, 0:depth] = q_ref[x]
        field[x + 1, rows:height, 0:depth] = yh_ref[x]
        field[x + 1, :, depth : depth + LANES] = zt_ref[x]
        return carry

    lax.fori_loop(0, planes, body, 0)


def stencil(src, x, coefs, rows, depth):
    height, width = src.shape[1:]
    strips = height // 8
    wanted = rows // 8
    row = lax.broadcasted_iota(jnp.int32, (8, depth), 0)
    tiles = {}
    ups = {}
    downs = {}

    def tile(t):
        t = t % strips
        if t not in tiles:
            tiles[t] = src[x + 1, 8 * t : 8 * t + 8, :]
        return tiles[t]

    def up(t):
        t = t % strips
        if t not in ups:
            ups[t] = pltpu.roll(tile(t)[:, :depth], 1, 0)
        return ups[t]

    def down(t):
        t = t % strips
        if t not in downs:
            downs[t] = pltpu.roll(tile(t)[:, :depth], 7, 0)
        return downs[t]

    results = []
    for t in range(wanted):
        part = pl.ds(8 * t, 8)

        def coef(index):
            return coefs[index][x, part, 0:depth]

        q = tile(t)
        total = coef(0) * q[:, :depth]
        total = total + coef(1) * src[x, part, 0:depth] + coef(2) * src[x + 2, part, 0:depth]
        total = total + coef(3) * jnp.where(row == 0, up(t - 1), up(t))
        total = total + coef(4) * jnp.where(row == 7, down(t + 1), down(t))
        total = total + coef(5) * pltpu.roll(q, 1, 1)[:, :depth]
        total = total + coef(6) * pltpu.roll(q, width - 1, 1)[:, :depth]
        results.append(total)
    return results


def transport_kernel(
    planes, modes_x, modes, v_ref, bx_ref, by_ref, bz_ref, q_ref, yh_ref, zt_ref, out_ref, *scratch
):
    field, middle = scratch[:2]
    coefs = scratch[2:]
    height, width = field.shape[1:]
    rows, depth = q_ref.shape[1:]
    gather_field(q_ref, yh_ref, zt_ref, field)
    middle[0] = jnp.zeros((height, width), F32)
    middle[planes + 1] = jnp.zeros((height, width), F32)
    expand_kernel(planes, modes_x, modes, v_ref, bx_ref, by_ref, bz_ref, coefs)

    def first(x, carry):
        for t, value in enumerate(stencil(field, x, coefs, height, width)):
            middle[x + 1, 8 * t : 8 * t + 8, :] = value
        return carry

    def second(x, carry):
        for t, value in enumerate(stencil(middle, x, coefs, height, width)):
            part = pl.ds(8 * t, 8)
            field[x + 1, part, :] = 0.5 * (field[x + 1, part, :] + value)
        return carry

    def last(x, carry):
        for t, value in enumerate(stencil(middle, x, coefs, rows, depth)):
            part = pl.ds(8 * t, 8)
            out_ref[x, part, :] = 0.5 * (field[x + 1, part, 0:depth] + value)
        return carry

    def step(i, carry):
        lax.fori_loop(0, planes, first, 0, unroll=4)
        lax.fori_loop(0, planes, second, 0, unroll=4)
        return carry

    lax.fori_loop(0, STEPS - 1, step, 0)
    lax.fori_loop(0, planes, first, 0, unroll=4)
    lax.fori_loop(0, planes, last, 0, unroll=4)


def project_kernel(
    planes, modes_x, adj_ref, q_ref, yh_ref, zt_ref, bx_ref, by_ref, bz_ref, out_ref, field, forcing, inner
):
    height, width = field.shape[1:]
    rows, depth = q_ref.shape[1:]
    gather_field(q_ref, yh_ref, zt_ref, field)
    by, bz = by_ref[lax.axis_index("ha")], bz_ref.at[lax.axis_index("dev")]

    def body(x, carry):
        plane = field[x + 1]
        half = 0.5 * adj_ref[x]
        slopes = (
            field[x + 2, 0:rows, 0:depth] - field[x, 0:rows, 0:depth],
            (pltpu.roll(plane, height - 1, 0) - pltpu.roll(plane, 1, 0))[0:rows, 0:depth],
            (pltpu.roll(plane, width - 1, 1) - pltpu.roll(plane, 1, 1))[0:rows, 0:depth],
        )
        for c in range(3):
            high, low = split(half * slopes[c])
            columns = slice(c * depth, (c + 1) * depth)
            forcing[pl.ds(x * 2 * rows, rows), columns] = high
            forcing[pl.ds(x * 2 * rows + rows, rows), columns] = low
        return carry

    lax.fori_loop(0, planes, body, 0)
    chunk = 8

    def multiply(i, carry):
        start = i * (chunk * 2 * rows)
        wide = jnp.dot(
            forcing[pl.ds(start, chunk * 2 * rows), :], bz[...], preferred_element_type=F32
        )
        wide = wide[:, 0:LANES] + wide[:, LANES : 2 * LANES]
        wide = wide.reshape(chunk, 2 * rows, LANES)
        inner[pl.ds(i * chunk, chunk)] = wide[:, 0:rows] + wide[:, rows : 2 * rows]
        return carry

    lax.fori_loop(0, planes // chunk, multiply, 0)

    def finish(a, carry):
        total = bx_ref[0, a] * inner[0]
        for x in range(1, planes):
            total = total + bx_ref[x, a] * inner[x]
        high, low = split(total)
        stacked = jnp.concatenate([high, low, high], axis=0)
        out_ref[a] = jnp.dot(by, stacked, preferred_element_type=F32)
        return carry

    lax.fori_loop(0, modes_x, finish, 0)


def peer_of(index, sides):
    return {"ha": index // sides, "dev": lax.rem(index, sides)}


MESH = pl.DeviceIdType.MESH


def halo_kernel(count_y, count_z, q_ref, yh_ref, zt_ref, left_ref, right_ref, send, recv):
    me_y, me_z = lax.axis_index("ha"), lax.axis_index("dev")
    rows, cols = q_ref.shape[1:]
    has = (me_y < count_y - 1, me_y > 0, me_z < count_z - 1, me_z > 0)
    peers = ({"ha": me_y + 1}, {"ha": me_y - 1}, {"dev": me_z + 1}, {"dev": me_z - 1})
    last = slice(cols - LANES, cols)
    first = slice(0, LANES)
    before, after = slice(HALO, 2 * HALO), slice(0, HALO)
    block, rim = slice(0, rows), slice(rows, rows + 2 * HALO)
    barrier = pltpu.get_barrier_semaphore()
    for there, peer in zip(has, peers):

        @pl.when(there)
        def _():
            pl.semaphore_signal(barrier, inc=1, device_id=peer, device_id_type=MESH)

    def copy(source, target, slot, peer):
        return pltpu.make_async_remote_copy(
            src_ref=source,
            dst_ref=target,
            send_sem=send.at[slot],
            recv_sem=recv.at[slot],
            device_id=peer,
            device_id_type=MESH,
        )

    for there, target in (
        (has[0], yh_ref.at[:, after]),
        (has[1], yh_ref.at[:, before]),
        (has[2], right_ref),
        (has[3], left_ref),
    ):

        @pl.when(jnp.logical_not(there))
        def _():
            target[...] = jnp.zeros(target.shape, F32)

    known = sum(jnp.where(there, 1, 0) for there in has)
    pl.semaphore_wait(barrier, known)

    rows_next = copy(q_ref.at[:, rows - HALO : rows], yh_ref.at[:, before], 0, peers[0])
    rows_prev = copy(q_ref.at[:, 0:HALO], yh_ref.at[:, after], 1, peers[1])
    tile_next = copy(q_ref.at[:, :, last], left_ref.at[:, block], 2, peers[2])
    tile_prev = copy(q_ref.at[:, :, first], right_ref.at[:, block], 3, peers[3])
    rim_next = copy(yh_ref.at[:, :, last], left_ref.at[:, rim], 4, peers[2])
    rim_prev = copy(yh_ref.at[:, :, first], right_ref.at[:, rim], 5, peers[3])

    def each(pairs):
        for there, action in pairs:

            @pl.when(there)
            def _():
                action()

    each(zip(has, [c.start for c in (rows_next, rows_prev, tile_next, tile_prev)]))
    each([(has[1], rows_next.wait_recv), (has[0], rows_prev.wait_recv)])
    each([(has[2], rim_next.start), (has[3], rim_prev.start)])
    each([(has[3], tile_next.wait_recv), (has[2], tile_prev.wait_recv)])
    each([(has[3], rim_next.wait_recv), (has[2], rim_prev.wait_recv)])
    lane = lax.broadcasted_iota(jnp.int32, zt_ref.shape[1:], 1)

    def merge(x, carry):
        zt_ref[x] = jnp.where(lane < LANES // 2, right_ref[x], left_ref[x])
        return carry

    lax.fori_loop(0, zt_ref.shape[0], merge, 0)
    each(zip(has, [c.wait_send for c in (rows_next, rows_prev, tile_next, tile_prev)]))
    each([(has[2], rim_next.wait_send), (has[3], rim_prev.wait_send)])


def update_kernel(count, sides, part_ref, old_ref, factor_ref, out_ref, held, send, recv, send2, recv2):
    me = lax.axis_index("ha") * sides + lax.axis_index("dev")
    rows = held.shape[1]
    barrier = pltpu.get_barrier_semaphore()
    for d in range(1, count):
        peer = lax.rem(me + d, count)
        pl.semaphore_signal(
            barrier, inc=1, device_id=peer_of(peer, sides), device_id_type=pl.DeviceIdType.MESH
        )
    pl.semaphore_wait(barrier, count - 1)
    mine = pl.ds(pl.multiple_of(me * rows, rows), rows)
    copies = []
    for d in range(1, count):
        peer = lax.rem(me + d, count)
        copy = pltpu.make_async_remote_copy(
            src_ref=part_ref.at[pl.ds(pl.multiple_of(peer * rows, rows), rows)],
            dst_ref=held.at[d],
            send_sem=send.at[d],
            recv_sem=recv.at[d],
            device_id=peer_of(peer, sides),
            device_id_type=pl.DeviceIdType.MESH,
        )
        copy.start()
        copies.append(copy)
    total = part_ref[mine]
    for d in range(1, count):
        copies[d - 1].wait_recv()
        total = total + held[d]
    out_ref[mine] = old_ref[mine] + factor_ref[mine] * total
    for copy in copies:
        copy.wait_send()
    copies = []
    for d in range(1, count):
        peer = lax.rem(me + d, count)
        copy = pltpu.make_async_remote_copy(
            src_ref=out_ref.at[mine],
            dst_ref=out_ref.at[mine],
            send_sem=send2.at[d],
            recv_sem=recv2.at[d],
            device_id=peer_of(peer, sides),
            device_id_type=pl.DeviceIdType.MESH,
        )
        copy.start()
        copies.append(copy)
    for copy in copies:
        copy.wait()


VMEM = pl.BlockSpec(memory_space=pltpu.VMEM)
SMEM = pl.BlockSpec(memory_space=pltpu.SMEM)
PARAMS = pltpu.CompilerParams(vmem_limit_bytes=60 * 1024 * 1024)


def halo_of(field):
    count = lax.axis_size("ha")
    forward = [(i, i + 1) for i in range(count - 1)]
    backward = [(i + 1, i) for i in range(count - 1)]
    before = lax.ppermute(field[:, -HALO:, :], "ha", forward)
    after = lax.ppermute(field[:, :HALO, :], "ha", backward)
    sides = lax.axis_size("dev")
    forward = [(i, i + 1) for i in range(sides - 1)]
    backward = [(i + 1, i) for i in range(sides - 1)]
    rows = jnp.concatenate([after, before], axis=1)
    head = jnp.concatenate([field[:, :, :HALO], rows[:, :, :HALO]], axis=1)
    tail = jnp.concatenate([field[:, :, -HALO:], rows[:, :, -HALO:]], axis=1)
    left = lax.ppermute(tail, "dev", forward)
    right = lax.ppermute(head, "dev", backward)
    gap = jnp.zeros(left.shape[:2] + (LANES - 2 * HALO,), F32)
    return rows, jnp.concatenate([right, gap, left], axis=2)


def per_device(brain_image, adjoint_field, velocity_modes):
    planes, rows, cols = brain_image.shape
    count_y = lax.axis_size("ha")
    count_z = lax.axis_size("dev")
    height, depth = rows * count_y, cols * count_z
    modes_x, modes = velocity_modes.shape[1:3]
    tall, wide = rows + 2 * HALO, cols + LANES

    expand_y, expand_z, project_y, project_z = [], [], [], []
    for i in range(count_y):
        high, low = halves(basis(wrapped(i * rows, rows, tall, height), height, modes))
        expand_y.append(np.concatenate([high, high, low], axis=1))
        high, low = high[:rows].T, low[:rows].T
        project_y.append(np.concatenate([high, high, low], axis=1))
    for i in range(count_z):
        high, low = halves(basis(wrapped(i * cols, cols, wide, depth), depth, modes))
        high, low = high.T, low.T
        table = np.zeros((LANES, wide), ml_dtypes.bfloat16)
        table[: 3 * modes] = np.concatenate([high, low, high], axis=0)
        expand_z.append(table)
        table = np.zeros((3, cols, 2, LANES), ml_dtypes.bfloat16)
        for c in range(3):
            table[c, :, 0, c * modes : (c + 1) * modes] = high.T[:cols]
            table[c, :, 1, c * modes : (c + 1) * modes] = low.T[:cols]
        project_z.append(table.reshape(3 * cols, 2 * LANES))

    by_wide, by_back = jnp.asarray(np.stack(expand_y)), jnp.asarray(np.stack(project_y))
    bz_wide, bz_back = jnp.asarray(np.stack(expand_z)), jnp.asarray(np.stack(project_z))
    bx = jnp.asarray(basis(np.arange(planes), planes, modes_x))
    factor = mode_factor((planes, height, depth), (modes_x, modes, modes))
    factor = np.tile(factor, (1, 1, LANES // modes)).astype(np.float32).reshape(-1, LANES)
    scale = 1.0 / math.sqrt(modes_x * modes * modes)

    def widen(value):
        return jnp.pad(value, ((0, 0), (0, 0), (0, LANES - 3 * modes)))

    plane = pltpu.VMEM((planes + 2, tall, wide), F32)
    transport = pl.pallas_call(
        functools.partial(transport_kernel, planes, modes_x, modes),
        out_shape=jax.ShapeDtypeStruct((planes, rows, cols), F32),
        in_specs=[VMEM, SMEM, VMEM, VMEM, VMEM, VMEM, VMEM],
        out_specs=VMEM,
        scratch_shapes=[plane, plane] + [pltpu.VMEM((planes, tall, wide), F32)] * 7,
        compiler_params=PARAMS,
        cost_estimate=pl.CostEstimate(
            flops=200 * planes * tall * wide, bytes_accessed=60_000_000, transcendentals=0
        ),
        name="transport",
    )
    project = pl.pallas_call(
        functools.partial(project_kernel, planes, modes_x),
        out_shape=jax.ShapeDtypeStruct((modes_x, modes, LANES), F32),
        in_specs=[VMEM, VMEM, VMEM, VMEM, SMEM, VMEM, VMEM],
        out_specs=VMEM,
        scratch_shapes=[
            plane,
            pltpu.VMEM((planes * 2 * rows, 3 * cols), BF16),
            pltpu.VMEM((planes, rows, LANES), F32),
        ],
        compiler_params=PARAMS,
        name="project",
    )

    devices = count_y * count_z
    entries = modes_x * modes
    update = pl.pallas_call(
        functools.partial(update_kernel, devices, count_z),
        out_shape=jax.ShapeDtypeStruct((entries, LANES), F32),
        in_specs=[VMEM, VMEM, VMEM],
        out_specs=VMEM,
        scratch_shapes=[pltpu.VMEM((devices, entries // devices, LANES), F32)]
        + [pltpu.SemaphoreType.DMA((devices,))] * 4,
        compiler_params=pltpu.CompilerParams(collective_id=0, has_side_effects=True),
        name="update",
    )

    sheet = jax.ShapeDtypeStruct((planes, tall, LANES), F32)
    halo = pl.pallas_call(
        functools.partial(halo_kernel, count_y, count_z),
        out_shape=(jax.ShapeDtypeStruct((planes, 2 * HALO, cols), F32), sheet),
        in_specs=[VMEM],
        out_specs=(VMEM, VMEM),
        scratch_shapes=[pltpu.VMEM(sheet.shape, F32)] * 2 + [pltpu.SemaphoreType.DMA((6,))] * 2,
        compiler_params=pltpu.CompilerParams(collective_id=1, has_side_effects=True),
        name="halo",
    )

    old = widen(velocity_modes.transpose(1, 2, 0, 3).reshape(modes_x, modes, 3 * modes))
    adjoint_halo = halo(adjoint_field)
    image_source, adjoint_halo = lax.optimization_barrier((brain_image, adjoint_halo))
    image_halo = halo_of(image_source)
    adjoint_end = transport(old, bx * -scale, by_wide, bz_wide, adjoint_field, *adjoint_halo)
    partial = project(adjoint_end, brain_image, *image_halo, bx, by_back, bz_back)
    updated = update(partial.reshape(entries, LANES), old.reshape(entries, LANES), factor)
    updated = updated.reshape(modes_x, modes, LANES)
    image_end = transport(updated, bx * scale, by_wide, bz_wide, brain_image, *image_halo)
    velocity_next = updated[:, :, : 3 * modes].reshape(modes_x, modes, 3, modes)
    velocity_next = velocity_next.transpose(2, 0, 1, 3)
    return (adjoint_end, image_end, velocity_next)


def solution(mesh):
    placed = (P("subj", "ha", "dev"), P("subj", "ha", "dev"), P("subj", None, None, None))
    return jax.shard_map(
        per_device,
        mesh=mesh,
        in_specs=placed,
        out_specs=placed,
        check_vma=False,
    )
```

```python
import functools
import math

import jax
import jax.numpy as jnp
import ml_dtypes
import numpy as np
from jax import lax
from jax.experimental import pallas as pl
from jax.experimental.pallas import tpu as pltpu
from jax.sharding import PartitionSpec as P

STEPS = 4
HALO = 2 * STEPS
STEP_SIZE = 4.0
STIFFNESS = 2.0
LANES = 128
F32 = jnp.float32
BF16 = jnp.bfloat16


def wavenumbers(modes):
    column = np.arange(modes)
    return np.where(column <= modes // 2, column, column - modes // 2)


def basis(positions, length, modes):
    phase = positions[:, None] * wavenumbers(modes)[None, :] % length
    angles = phase * (2.0 * math.pi / length)
    cosine = np.arange(modes)[None, :] <= modes // 2
    table = np.where(cosine, np.cos(angles), np.sin(angles))
    inside = (positions >= 0) & (positions < length)
    return np.where(inside[:, None], table, 0.0).astype(np.float32)


def halves(table):
    high = table.astype(ml_dtypes.bfloat16)
    low = (table - high.astype(np.float32)).astype(ml_dtypes.bfloat16)
    return high, low


def wrapped(start, rows, total, length):
    gap = np.full(total - rows - 2 * HALO, -1)
    after = np.arange(start + rows, start + rows + HALO)
    before = np.arange(start - HALO, start)
    return np.concatenate([np.arange(start, start + rows), after, gap, before])


def mode_factor(lengths, modes):
    eigen, weight = [], []
    for length, count in zip(lengths, modes):
        eigen.append(2.0 - 2.0 * np.cos(wavenumbers(count) * (2.0 * math.pi / length)))
        weight.append(np.where(np.arange(count) == 0, length, length / 2.0))
    value = eigen[0][:, None, None] + eigen[1][None, :, None] + eigen[2][None, None, :]
    norm = weight[0][:, None, None] * weight[1][None, :, None] * weight[2][None, None, :]
    return STEP_SIZE * math.sqrt(math.prod(modes)) / (norm * (1.0 + STIFFNESS * value) ** 2)


def split(value):
    high = value.astype(BF16)
    return high, (value - high.astype(F32)).astype(BF16)


def expand_kernel(planes, modes_x, modes, v_ref, bx_ref, by_ref, bz_ref, coefs):
    height, depth = coefs[0].shape[1:]
    by, bz = by_ref[lax.axis_index("ha")], bz_ref.at[lax.axis_index("dev")]
    group = lax.broadcasted_iota(jnp.int32, (height, LANES), 1) // modes

    def body(x, carry):
        weighted = bx_ref[x, 0] * v_ref[0]
        for a in range(1, modes_x):
            weighted = weighted + bx_ref[x, a] * v_ref[a]
        high, low = split(weighted)
        rows = jnp.concatenate([high, low, high], axis=0)
        mixed = jnp.dot(by, rows, preferred_element_type=F32)
        top = mixed.astype(BF16).astype(F32)
        rest = mixed - top
        total = jnp.ones((height, depth), F32)
        for c in range(3):
            first = pltpu.roll(top, (-c * modes) % LANES, 1) if c else top
            second = pltpu.roll(top, ((1 - c) * modes) % LANES, 1) if c != 1 else top
            third = pltpu.roll(rest, ((2 - c) * modes) % LANES, 1) if c != 2 else rest
            left = jnp.where(group == 0, first, jnp.where(group == 1, second, third))
            speed = jnp.dot(left.astype(BF16), bz[...], preferred_element_type=F32)
            plus = jnp.maximum(speed, 0.0)
            minus = jnp.maximum(-speed, 0.0)
            coefs[1 + 2 * c][x] = plus
            coefs[2 + 2 * c][x] = minus
            total = total - (plus + minus)
        coefs[0][x] = total
        return carry

    lax.fori_loop(0, planes, body, 0, unroll=2)


def gather_field(q_ref, yh_ref, tile, field):
    planes, rows, depth = q_ref.shape
    height = field.shape[1]
    field[0] = jnp.zeros(field.shape[1:], F32)
    field[planes + 1] = jnp.zeros(field.shape[1:], F32)

    def body(x, carry):
        field[x + 1, 0:rows, 0:depth] = q_ref[x]
        field[x + 1, rows:height, 0:depth] = yh_ref[x]
        field[x + 1, :, depth : depth + LANES] = tile(x)
        return carry

    lax.fori_loop(0, planes, body, 0)


def stencil(src, x, coefs, rows, depth):
    height, width = src.shape[1:]
    strips = height // 8
    wanted = rows // 8
    row = lax.broadcasted_iota(jnp.int32, (8, depth), 0)
    tiles = {}
    ups = {}
    downs = {}

    def tile(t):
        t = t % strips
        if t not in tiles:
            tiles[t] = src[x + 1, 8 * t : 8 * t + 8, :]
        return tiles[t]

    def up(t):
        t = t % strips
        if t not in ups:
            ups[t] = pltpu.roll(tile(t)[:, :depth], 1, 0)
        return ups[t]

    def down(t):
        t = t % strips
        if t not in downs:
            downs[t] = pltpu.roll(tile(t)[:, :depth], 7, 0)
        return downs[t]

    results = []
    for t in range(wanted):
        part = pl.ds(8 * t, 8)

        def coef(index):
            return coefs[index][x, part, 0:depth]

        q = tile(t)
        total = coef(0) * q[:, :depth]
        total = total + coef(1) * src[x, part, 0:depth] + coef(2) * src[x + 2, part, 0:depth]
        total = total + coef(3) * jnp.where(row == 0, up(t - 1), up(t))
        total = total + coef(4) * jnp.where(row == 7, down(t + 1), down(t))
        total = total + coef(5) * pltpu.roll(q, 1, 1)[:, :depth]
        total = total + coef(6) * pltpu.roll(q, width - 1, 1)[:, :depth]
        results.append(total)
    return results


def transport(planes, q_ref, out_ref, field, middle, coefs, between):
    height, width = field.shape[1:]
    rows, depth = q_ref.shape[1:]

    def first(x, carry):
        for t, value in enumerate(stencil(field, x, coefs, height, width)):
            middle[x + 1, 8 * t : 8 * t + 8, :] = value
        return carry

    def second(x, carry):
        for t, value in enumerate(stencil(middle, x, coefs, height, width)):
            part = pl.ds(8 * t, 8)
            field[x + 1, part, :] = 0.5 * (field[x + 1, part, :] + value)
        return carry

    def last(x, carry):
        for t, value in enumerate(stencil(middle, x, coefs, rows, depth)):
            part = pl.ds(8 * t, 8)
            out_ref[x, part, :] = 0.5 * (field[x + 1, part, 0:depth] + value)
        return carry

    def step(i, carry):
        lax.fori_loop(0, planes, first, 0, unroll=4)
        lax.fori_loop(0, planes, second, 0, unroll=4)
        return carry

    lax.fori_loop(0, STEPS - 1, step, 0)
    between()
    lax.fori_loop(0, planes, first, 0, unroll=4)
    lax.fori_loop(0, planes, last, 0, unroll=4)


def adjoint_kernel(
    planes, modes_x, modes, count_y, count_z, v_ref, bx_ref, by_ref, bz_ref, q_ref, image_ref,
    out_ref, image_yh, image_zt, yh_ref, left, right, image_left, image_right,
    send, recv, image_send, image_recv, field, middle, *coefs
):
    has, peers = neighbours(count_y, count_z)
    mine = Exchange(has, peers, q_ref, yh_ref, left, right, send, recv)
    image = Exchange(
        has, peers, image_ref, image_yh, image_left, image_right, image_send, image_recv
    )
    mine.clear()
    image.clear()
    greet(has, peers)
    mine.start()
    middle[0] = jnp.zeros(middle.shape[1:], F32)
    middle[planes + 1] = jnp.zeros(middle.shape[1:], F32)
    expand_kernel(planes, modes_x, modes, v_ref, bx_ref, by_ref, bz_ref, coefs)
    mine.forward()
    image.start()
    mine.finish()
    gather_field(q_ref, yh_ref, mine.tile, field)
    transport(planes, q_ref, out_ref, field, middle, coefs, image.forward)
    image.finish()

    def merge(x, carry):
        image_zt[x] = image.tile(x)
        return carry

    lax.fori_loop(0, planes, merge, 0)


def image_kernel(
    planes, modes_x, modes, v_ref, bx_ref, by_ref, bz_ref, q_ref, yh_ref, zt_ref,
    out_ref, next_ref, field, middle, *coefs
):
    for c in range(3):
        for a in range(modes_x):
            next_ref[c, a] = v_ref[a][:, c * modes : (c + 1) * modes]
    middle[0] = jnp.zeros(middle.shape[1:], F32)
    middle[planes + 1] = jnp.zeros(middle.shape[1:], F32)
    gather_field(q_ref, yh_ref, lambda x: zt_ref[x], field)
    expand_kernel(planes, modes_x, modes, v_ref, bx_ref, by_ref, bz_ref, coefs)
    transport(planes, q_ref, out_ref, field, middle, coefs, lambda: None)


def project_kernel(
    planes, modes_x, adj_ref, q_ref, yh_ref, zt_ref, bx_ref, by_ref, bz_ref, out_ref, field, forcing, inner
):
    height, width = field.shape[1:]
    rows, depth = q_ref.shape[1:]
    gather_field(q_ref, yh_ref, lambda x: zt_ref[x], field)
    by, bz = by_ref[lax.axis_index("ha")], bz_ref.at[lax.axis_index("dev")]

    def body(x, carry):
        plane = field[x + 1]
        half = 0.5 * adj_ref[x]
        slopes = (
            field[x + 2, 0:rows, 0:depth] - field[x, 0:rows, 0:depth],
            (pltpu.roll(plane, height - 1, 0) - pltpu.roll(plane, 1, 0))[0:rows, 0:depth],
            (pltpu.roll(plane, width - 1, 1) - pltpu.roll(plane, 1, 1))[0:rows, 0:depth],
        )
        for c in range(3):
            high, low = split(half * slopes[c])
            columns = slice(c * depth, (c + 1) * depth)
            forcing[pl.ds(x * 2 * rows, rows), columns] = high
            forcing[pl.ds(x * 2 * rows + rows, rows), columns] = low
        return carry

    lax.fori_loop(0, planes, body, 0)
    chunk = 8

    def multiply(i, carry):
        start = i * (chunk * 2 * rows)
        wide = jnp.dot(
            forcing[pl.ds(start, chunk * 2 * rows), :], bz[...], preferred_element_type=F32
        )
        wide = wide[:, 0:LANES] + wide[:, LANES : 2 * LANES]
        wide = wide.reshape(chunk, 2 * rows, LANES)
        inner[pl.ds(i * chunk, chunk)] = wide[:, 0:rows] + wide[:, rows : 2 * rows]
        return carry

    lax.fori_loop(0, planes // chunk, multiply, 0)

    def finish(a, carry):
        total = bx_ref[0, a] * inner[0]
        for x in range(1, planes):
            total = total + bx_ref[x, a] * inner[x]
        high, low = split(total)
        stacked = jnp.concatenate([high, low, high], axis=0)
        out_ref[a] = jnp.dot(by, stacked, preferred_element_type=F32)
        return carry

    lax.fori_loop(0, modes_x, finish, 0)


def peer_of(index, sides):
    return {"ha": index // sides, "dev": lax.rem(index, sides)}


MESH = pl.DeviceIdType.MESH


def neighbours(count_y, count_z):
    me_y, me_z = lax.axis_index("ha"), lax.axis_index("dev")
    has = (me_y < count_y - 1, me_y > 0, me_z < count_z - 1, me_z > 0)
    peers = ({"ha": me_y + 1}, {"ha": me_y - 1}, {"dev": me_z + 1}, {"dev": me_z - 1})
    return has, peers


def each(pairs):
    for there, action in pairs:

        @pl.when(there)
        def _():
            action()


def greet(has, peers):
    barrier = pltpu.get_barrier_semaphore()
    for there, peer in zip(has, peers):

        @pl.when(there)
        def _():
            pl.semaphore_signal(barrier, inc=1, device_id=peer, device_id_type=MESH)

    pl.semaphore_wait(barrier, sum(jnp.where(there, 1, 0) for there in has))


class Exchange:
    def __init__(self, has, peers, q_ref, yh_ref, left_ref, right_ref, send, recv):
        rows, cols = q_ref.shape[1:]
        last = slice(cols - LANES, cols)
        first = slice(0, LANES)
        before, after = slice(HALO, 2 * HALO), slice(0, HALO)
        block, rim = slice(0, rows), slice(rows, rows + 2 * HALO)

        def copy(source, target, slot, peer):
            return pltpu.make_async_remote_copy(
                src_ref=source,
                dst_ref=target,
                send_sem=send.at[slot],
                recv_sem=recv.at[slot],
                device_id=peer,
                device_id_type=MESH,
            )

        self.has = has
        self.sides = left_ref, right_ref
        self.targets = yh_ref.at[:, after], yh_ref.at[:, before], right_ref, left_ref
        self.blocks = (
            copy(q_ref.at[:, rows - HALO : rows], yh_ref.at[:, before], 0, peers[0]),
            copy(q_ref.at[:, 0:HALO], yh_ref.at[:, after], 1, peers[1]),
            copy(q_ref.at[:, :, last], left_ref.at[:, block], 2, peers[2]),
            copy(q_ref.at[:, :, first], right_ref.at[:, block], 3, peers[3]),
        )
        self.rims = (
            copy(yh_ref.at[:, :, last], left_ref.at[:, rim], 4, peers[2]),
            copy(yh_ref.at[:, :, first], right_ref.at[:, rim], 5, peers[3]),
        )

    def clear(self):
        for there, target in zip(self.has, self.targets):

            @pl.when(jnp.logical_not(there))
            def _():
                target[...] = jnp.zeros(target.shape, F32)

    def start(self):
        each(zip(self.has, [copy.start for copy in self.blocks]))

    def forward(self):
        up, down, right, left = self.has
        each([(down, self.blocks[0].wait_recv), (up, self.blocks[1].wait_recv)])
        each([(right, self.rims[0].start), (left, self.rims[1].start)])

    def finish(self):
        up, down, right, left = self.has
        each([(left, self.blocks[2].wait_recv), (right, self.blocks[3].wait_recv)])
        each([(left, self.rims[0].wait_recv), (right, self.rims[1].wait_recv)])
        each(zip(self.has, [copy.wait_send for copy in self.blocks]))
        each([(right, self.rims[0].wait_send), (left, self.rims[1].wait_send)])

    def tile(self, x):
        left_ref, right_ref = self.sides
        lane = lax.broadcasted_iota(jnp.int32, left_ref.shape[1:], 1)
        return jnp.where(lane < LANES // 2, right_ref[x], left_ref[x])


def update_kernel(count, sides, part_ref, old_ref, factor_ref, out_ref, held, send, recv, send2, recv2):
    me = lax.axis_index("ha") * sides + lax.axis_index("dev")
    rows = held.shape[1]
    barrier = pltpu.get_barrier_semaphore()
    for d in range(1, count):
        peer = lax.rem(me + d, count)
        pl.semaphore_signal(
            barrier, inc=1, device_id=peer_of(peer, sides), device_id_type=pl.DeviceIdType.MESH
        )
    pl.semaphore_wait(barrier, count - 1)
    mine = pl.ds(pl.multiple_of(me * rows, rows), rows)
    copies = []
    for d in range(1, count):
        peer = lax.rem(me + d, count)
        copy = pltpu.make_async_remote_copy(
            src_ref=part_ref.at[pl.ds(pl.multiple_of(peer * rows, rows), rows)],
            dst_ref=held.at[d],
            send_sem=send.at[d],
            recv_sem=recv.at[d],
            device_id=peer_of(peer, sides),
            device_id_type=pl.DeviceIdType.MESH,
        )
        copy.start()
        copies.append(copy)
    total = part_ref[mine]
    for d in range(1, count):
        copies[d - 1].wait_recv()
        total = total + held[d]
    out_ref[mine] = old_ref[mine] + factor_ref[mine] * total
    for copy in copies:
        copy.wait_send()
    copies = []
    for d in range(1, count):
        peer = lax.rem(me + d, count)
        copy = pltpu.make_async_remote_copy(
            src_ref=out_ref.at[mine],
            dst_ref=out_ref.at[mine],
            send_sem=send2.at[d],
            recv_sem=recv2.at[d],
            device_id=peer_of(peer, sides),
            device_id_type=pl.DeviceIdType.MESH,
        )
        copy.start()
        copies.append(copy)
    for copy in copies:
        copy.wait()


VMEM = pl.BlockSpec(memory_space=pltpu.VMEM)
SMEM = pl.BlockSpec(memory_space=pltpu.SMEM)
PARAMS = pltpu.CompilerParams(vmem_limit_bytes=60 * 1024 * 1024)


def per_device(brain_image, adjoint_field, velocity_modes):
    planes, rows, cols = brain_image.shape
    count_y = lax.axis_size("ha")
    count_z = lax.axis_size("dev")
    height, depth = rows * count_y, cols * count_z
    modes_x, modes = velocity_modes.shape[1:3]
    tall, wide = rows + 2 * HALO, cols + LANES

    expand_y, expand_z, project_y, project_z = [], [], [], []
    for i in range(count_y):
        high, low = halves(basis(wrapped(i * rows, rows, tall, height), height, modes))
        expand_y.append(np.concatenate([high, high, low], axis=1))
        high, low = high[:rows].T, low[:rows].T
        project_y.append(np.concatenate([high, high, low], axis=1))
    for i in range(count_z):
        high, low = halves(basis(wrapped(i * cols, cols, wide, depth), depth, modes))
        high, low = high.T, low.T
        table = np.zeros((LANES, wide), ml_dtypes.bfloat16)
        table[: 3 * modes] = np.concatenate([high, low, high], axis=0)
        expand_z.append(table)
        table = np.zeros((3, cols, 2, LANES), ml_dtypes.bfloat16)
        for c in range(3):
            table[c, :, 0, c * modes : (c + 1) * modes] = high.T[:cols]
            table[c, :, 1, c * modes : (c + 1) * modes] = low.T[:cols]
        project_z.append(table.reshape(3 * cols, 2 * LANES))

    by_wide, by_back = jnp.asarray(np.stack(expand_y)), jnp.asarray(np.stack(project_y))
    bz_wide, bz_back = jnp.asarray(np.stack(expand_z)), jnp.asarray(np.stack(project_z))
    bx = jnp.asarray(basis(np.arange(planes), planes, modes_x))
    factor = mode_factor((planes, height, depth), (modes_x, modes, modes))
    factor = np.tile(factor, (1, 1, LANES // modes)).astype(np.float32).reshape(-1, LANES)
    scale = 1.0 / math.sqrt(modes_x * modes * modes)

    def widen(value):
        return jnp.pad(value, ((0, 0), (0, 0), (0, LANES - 3 * modes)))

    plane = pltpu.VMEM((planes + 2, tall, wide), F32)
    block = jax.ShapeDtypeStruct((planes, rows, cols), F32)
    rims = jax.ShapeDtypeStruct((planes, 2 * HALO, cols), F32)
    sheet = jax.ShapeDtypeStruct((planes, tall, LANES), F32)
    work = [plane, plane] + [pltpu.VMEM((planes, tall, wide), F32)] * 7
    adjoint_transport = pl.pallas_call(
        functools.partial(adjoint_kernel, planes, modes_x, modes, count_y, count_z),
        out_shape=(block, rims, sheet),
        in_specs=[VMEM, SMEM, VMEM, VMEM, VMEM, VMEM],
        out_specs=(VMEM, VMEM, VMEM),
        scratch_shapes=[pltpu.VMEM(rims.shape, F32)]
        + [pltpu.VMEM(sheet.shape, F32)] * 4
        + [pltpu.SemaphoreType.DMA((6,))] * 4
        + work,
        compiler_params=pltpu.CompilerParams(
            vmem_limit_bytes=60 * 1024 * 1024, collective_id=1, has_side_effects=True
        ),
        name="adjoint_transport",
    )
    image_transport = pl.pallas_call(
        functools.partial(image_kernel, planes, modes_x, modes),
        out_shape=(block, jax.ShapeDtypeStruct(velocity_modes.shape, F32)),
        in_specs=[VMEM, SMEM, VMEM, VMEM, VMEM, VMEM, VMEM],
        out_specs=(VMEM, VMEM),
        scratch_shapes=work,
        compiler_params=PARAMS,
        name="image_transport",
    )
    project = pl.pallas_call(
        functools.partial(project_kernel, planes, modes_x),
        out_shape=jax.ShapeDtypeStruct((modes_x, modes, LANES), F32),
        in_specs=[VMEM, VMEM, VMEM, VMEM, SMEM, VMEM, VMEM],
        out_specs=VMEM,
        scratch_shapes=[
            plane,
            pltpu.VMEM((planes * 2 * rows, 3 * cols), BF16),
            pltpu.VMEM((planes, rows, LANES), F32),
        ],
        compiler_params=PARAMS,
        name="project",
    )

    devices = count_y * count_z
    entries = modes_x * modes
    update = pl.pallas_call(
        functools.partial(update_kernel, devices, count_z),
        out_shape=jax.ShapeDtypeStruct((entries, LANES), F32),
        in_specs=[VMEM, VMEM, VMEM],
        out_specs=VMEM,
        scratch_shapes=[pltpu.VMEM((devices, entries // devices, LANES), F32)]
        + [pltpu.SemaphoreType.DMA((devices,))] * 4,
        compiler_params=pltpu.CompilerParams(collective_id=0, has_side_effects=True),
        name="update",
    )

    old = widen(velocity_modes.transpose(1, 2, 0, 3).reshape(modes_x, modes, 3 * modes))
    adjoint_end, *image_halo = adjoint_transport(
        old, bx * -scale, by_wide, bz_wide, adjoint_field, brain_image
    )
    partial = project(adjoint_end, brain_image, *image_halo, bx, by_back, bz_back)
    updated = update(partial.reshape(entries, LANES), old.reshape(entries, LANES), factor)
    image_end, velocity_next = image_transport(
        updated.reshape(modes_x, modes, LANES),
        bx * scale,
        by_wide,
        bz_wide,
        brain_image,
        *image_halo,
    )
    return (adjoint_end, image_end, velocity_next)


def solution(mesh):
    placed = (P("subj", "ha", "dev"), P("subj", "ha", "dev"), P("subj", None, None, None))
    return jax.shard_map(
        per_device,
        mesh=mesh,
        in_specs=placed,
        out_specs=placed,
        check_vma=False,
    )
```

```python
import functools
import math

import jax
import jax.numpy as jnp
import ml_dtypes
import numpy as np
from jax import lax
from jax.experimental import pallas as pl
from jax.experimental.pallas import tpu as pltpu
from jax.sharding import PartitionSpec as P

STEPS = 4
HALO = 2 * STEPS
STEP_SIZE = 4.0
STIFFNESS = 2.0
LANES = 128
F32 = jnp.float32
BF16 = jnp.bfloat16


def wavenumbers(modes):
    column = np.arange(modes)
    return np.where(column <= modes // 2, column, column - modes // 2)


def basis(positions, length, modes):
    phase = positions[:, None] * wavenumbers(modes)[None, :] % length
    angles = phase * (2.0 * math.pi / length)
    cosine = np.arange(modes)[None, :] <= modes // 2
    table = np.where(cosine, np.cos(angles), np.sin(angles))
    inside = (positions >= 0) & (positions < length)
    return np.where(inside[:, None], table, 0.0).astype(np.float32)


def halves(table):
    high = table.astype(ml_dtypes.bfloat16)
    low = (table - high.astype(np.float32)).astype(ml_dtypes.bfloat16)
    return high, low


def wrapped(start, rows, total, length):
    gap = np.full(total - rows - 2 * HALO, -1)
    after = np.arange(start + rows, start + rows + HALO)
    before = np.arange(start - HALO, start)
    return np.concatenate([np.arange(start, start + rows), after, gap, before])


def mode_factor(lengths, modes):
    eigen, weight = [], []
    for length, count in zip(lengths, modes):
        eigen.append(2.0 - 2.0 * np.cos(wavenumbers(count) * (2.0 * math.pi / length)))
        weight.append(np.where(np.arange(count) == 0, length, length / 2.0))
    value = eigen[0][:, None, None] + eigen[1][None, :, None] + eigen[2][None, None, :]
    norm = weight[0][:, None, None] * weight[1][None, :, None] * weight[2][None, None, :]
    return STEP_SIZE * math.sqrt(math.prod(modes)) / (norm * (1.0 + STIFFNESS * value) ** 2)


def split(value):
    high = value.astype(BF16)
    return high, (value - high.astype(F32)).astype(BF16)


def expand_kernel(planes, modes_x, modes, v_ref, bx_ref, by_ref, bz_ref, coefs):
    height, depth = coefs[0].shape[1:]
    by, bz = by_ref[lax.axis_index("ha")], bz_ref.at[lax.axis_index("dev")]
    group = lax.broadcasted_iota(jnp.int32, (height, LANES), 1) // modes

    def body(x, carry):
        weighted = bx_ref[x, 0] * v_ref[0]
        for a in range(1, modes_x):
            weighted = weighted + bx_ref[x, a] * v_ref[a]
        high, low = split(weighted)
        rows = jnp.concatenate([high, low, high], axis=0)
        mixed = jnp.dot(by, rows, preferred_element_type=F32)
        top = mixed.astype(BF16).astype(F32)
        rest = mixed - top
        total = jnp.ones((height, depth), F32)
        for c in range(3):
            first = pltpu.roll(top, (-c * modes) % LANES, 1) if c else top
            second = pltpu.roll(top, ((1 - c) * modes) % LANES, 1) if c != 1 else top
            third = pltpu.roll(rest, ((2 - c) * modes) % LANES, 1) if c != 2 else rest
            left = jnp.where(group == 0, first, jnp.where(group == 1, second, third))
            speed = jnp.dot(left.astype(BF16), bz[...], preferred_element_type=F32)
            plus = jnp.maximum(speed, 0.0)
            minus = jnp.maximum(-speed, 0.0)
            coefs[1 + 2 * c][x] = plus
            coefs[2 + 2 * c][x] = minus
            total = total - (plus + minus)
        coefs[0][x] = total
        return carry

    lax.fori_loop(0, planes, body, 0, unroll=2)


def gather_field(q_ref, yh_ref, tile, field):
    tiles, height = field.shape[0], field.shape[2]
    planes, rows, depth = q_ref.shape
    edge = jnp.zeros((height, LANES), F32)
    spare = jnp.zeros((HALO, LANES), F32)
    block = slice(2 * HALO, 2 * HALO + rows)
    after = slice(2 * HALO + rows, 3 * HALO + rows)
    before = slice(HALO, 2 * HALO)
    for t in range(tiles):
        field[t, 0] = edge
        field[t, planes + 1] = edge

    def body(x, carry):
        side = tile(x)
        for t in range(tiles):
            lanes = slice(t * LANES, (t + 1) * LANES)
            field[t, x + 1, 0:HALO] = spare
            field[t, x + 1, height - HALO : height] = spare
            last = t == tiles - 1
            field[t, x + 1, block] = side[0:rows] if last else q_ref[x, :, lanes]
            field[t, x + 1, after] = (
                side[rows : rows + HALO] if last else yh_ref[x, 0:HALO, lanes]
            )
            field[t, x + 1, before] = (
                side[rows + HALO :] if last else yh_ref[x, HALO : 2 * HALO, lanes]
            )
        return carry

    lax.fori_loop(0, planes, body, 0)


def clear_edges(middle):
    tiles, planes, height = middle.shape[:3]
    edge = jnp.zeros((height, LANES), F32)
    spare = jnp.zeros((HALO, LANES), F32)
    for t in range(tiles):
        middle[t, 0] = edge
        middle[t, planes - 1] = edge

    def body(x, carry):
        for t in range(tiles):
            middle[t, x, 0:HALO] = spare
            middle[t, x, height - HALO : height] = spare
        return carry

    lax.fori_loop(0, planes, body, 0)


def stencil(src, start, group, coefs, strips, tiles):
    lane = lax.broadcasted_iota(jnp.int32, (8, LANES), 1)
    count = src.shape[0]
    for t in strips:
        row = HALO + 8 * t
        planes = [
            [src[k, start + i, row : row + 8] for k in range(count)] for i in range(group + 2)
        ]
        for i in range(group):
            x = start + i
            here = planes[i + 1]
            ahead = [pltpu.roll(value, 1, 1) for value in here]
            back = [pltpu.roll(value, LANES - 1, 1) for value in here]
            for k in range(tiles):

                def coef(index):
                    return coefs[index][x, 8 * t : 8 * t + 8, k * LANES : (k + 1) * LANES]

                total = coef(0) * here[k]
                total = total + (coef(1) * planes[i][k] + coef(2) * planes[i + 2][k])
                total = total + (
                    coef(3) * src[k, x + 1, row - 1 : row + 7]
                    + coef(4) * src[k, x + 1, row + 1 : row + 9]
                )
                left = jnp.where(lane == 0, ahead[k - 1], ahead[k])
                right = jnp.where(lane == LANES - 1, back[(k + 1) % count], back[k])
                yield x, t, k, total + (coef(5) * left + coef(6) * right)


def transport(planes, q_ref, out_ref, field, middle, coefs, between):
    tiles = field.shape[0]
    rows, depth = q_ref.shape[1:]
    strips = (rows + 2 * HALO) // 8
    scale = 0.5**STEPS

    group = math.gcd(planes, 4)

    def first(i, carry):
        for x, t, k, value in stencil(field, group * i, group, coefs, range(strips), tiles):
            middle[k, x + 1, HALO + 8 * t : HALO + 8 * t + 8] = value
        return carry

    def second(i, carry):
        for x, t, k, value in stencil(middle, group * i, group, coefs, range(strips), tiles):
            part = slice(HALO + 8 * t, HALO + 8 * t + 8)
            field[k, x + 1, part] = field[k, x + 1, part] + value
        return carry

    def last(i, carry):
        inner = range(HALO // 8, strips - HALO // 8)
        for x, t, k, value in stencil(middle, group * i, group, coefs, inner, depth // LANES):
            part = slice(HALO + 8 * t, HALO + 8 * t + 8)
            lanes = slice(k * LANES, (k + 1) * LANES)
            row = 8 * t - HALO
            out_ref[x, row : row + 8, lanes] = scale * (field[k, x + 1, part] + value)
        return carry

    def step(i, carry):
        lax.fori_loop(0, planes // group, first, 0, unroll=2)
        lax.fori_loop(0, planes // group, second, 0, unroll=2)
        return carry

    lax.fori_loop(0, STEPS - 1, step, 0)
    between()
    lax.fori_loop(0, planes // group, first, 0, unroll=2)
    lax.fori_loop(0, planes // group, last, 0, unroll=2)


def adjoint_kernel(
    planes, modes_x, modes, count_y, count_z, v_ref, bx_ref, by_ref, bz_ref, q_ref, image_ref,
    out_ref, image_yh, image_zt, yh_ref, left, right, image_left, image_right,
    send, recv, image_send, image_recv, field, middle, *coefs
):
    has, peers = neighbours(count_y, count_z)
    mine = Exchange(has, peers, q_ref, yh_ref, left, right, send, recv)
    image = Exchange(
        has, peers, image_ref, image_yh, image_left, image_right, image_send, image_recv
    )
    mine.clear()
    image.clear()
    greet(has, peers)
    mine.start()
    clear_edges(middle)
    expand_kernel(planes, modes_x, modes, v_ref, bx_ref, by_ref, bz_ref, coefs)
    mine.forward()
    image.start()
    mine.finish()
    gather_field(q_ref, yh_ref, mine.tile, field)
    transport(planes, q_ref, out_ref, field, middle, coefs, image.forward)
    image.finish()

    def merge(x, carry):
        image_zt[x] = image.tile(x)
        return carry

    lax.fori_loop(0, planes, merge, 0)


def image_kernel(
    planes, modes_x, modes, v_ref, bx_ref, by_ref, bz_ref, q_ref, yh_ref, zt_ref,
    out_ref, next_ref, field, middle, *coefs
):
    for c in range(3):
        for a in range(modes_x):
            next_ref[c, a] = v_ref[a][:, c * modes : (c + 1) * modes]
    clear_edges(middle)
    gather_field(q_ref, yh_ref, lambda x: zt_ref[x], field)
    expand_kernel(planes, modes_x, modes, v_ref, bx_ref, by_ref, bz_ref, coefs)
    transport(planes, q_ref, out_ref, field, middle, coefs, lambda: None)


def project_kernel(
    planes, modes_x, adj_ref, q_ref, yh_ref, zt_ref, bx_ref, by_ref, bz_ref, out_ref, field, forcing, inner
):
    rows, depth = q_ref.shape[1:]
    tiles = field.shape[0]
    gather_field(q_ref, yh_ref, lambda x: zt_ref[x], field)
    by, bz = by_ref[lax.axis_index("ha")], bz_ref.at[lax.axis_index("dev")]
    start = 2 * HALO

    def body(x, carry):
        half = 0.5 * adj_ref[x]

        def take(plane, offset):
            part = slice(start + offset, start + offset + rows)
            parts = [field[k, plane, part] for k in range(depth // LANES)]
            return jnp.concatenate(parts, axis=1)

        row = jnp.concatenate([field[k, x + 1, start : start + rows] for k in range(tiles)], axis=1)
        width = tiles * LANES
        slopes = (
            take(x + 2, 0) - take(x, 0),
            take(x + 1, 1) - take(x + 1, -1),
            (pltpu.roll(row, width - 1, 1) - pltpu.roll(row, 1, 1))[:, 0:depth],
        )
        for c in range(3):
            high, low = split(half * slopes[c])
            columns = slice(c * depth, (c + 1) * depth)
            forcing[pl.ds(x * 2 * rows, rows), columns] = high
            forcing[pl.ds(x * 2 * rows + rows, rows), columns] = low
        return carry

    lax.fori_loop(0, planes, body, 0, unroll=2)
    chunk = 8

    def multiply(i, carry):
        start = i * (chunk * 2 * rows)
        wide = jnp.dot(
            forcing[pl.ds(start, chunk * 2 * rows), :], bz[...], preferred_element_type=F32
        )
        wide = wide[:, 0:LANES] + wide[:, LANES : 2 * LANES]
        wide = wide.reshape(chunk, 2 * rows, LANES)
        inner[pl.ds(i * chunk, chunk)] = wide[:, 0:rows] + wide[:, rows : 2 * rows]
        return carry

    lax.fori_loop(0, planes // chunk, multiply, 0)

    def finish(a, carry):
        total = bx_ref[0, a] * inner[0]
        for x in range(1, planes):
            total = total + bx_ref[x, a] * inner[x]
        high, low = split(total)
        stacked = jnp.concatenate([high, low, high], axis=0)
        out_ref[a] = jnp.dot(by, stacked, preferred_element_type=F32)
        return carry

    lax.fori_loop(0, modes_x, finish, 0, unroll=2)


MESH = pl.DeviceIdType.MESH


def neighbours(count_y, count_z):
    me_y, me_z = lax.axis_index("ha"), lax.axis_index("dev")
    has = (me_y < count_y - 1, me_y > 0, me_z < count_z - 1, me_z > 0)
    peers = ({"ha": me_y + 1}, {"ha": me_y - 1}, {"dev": me_z + 1}, {"dev": me_z - 1})
    return has, peers


def each(pairs):
    for there, action in pairs:

        @pl.when(there)
        def _():
            action()


def greet(has, peers):
    barrier = pltpu.get_barrier_semaphore()
    for there, peer in zip(has, peers):

        @pl.when(there)
        def _():
            pl.semaphore_signal(barrier, inc=1, device_id=peer, device_id_type=MESH)

    pl.semaphore_wait(barrier, sum(jnp.where(there, 1, 0) for there in has))


class Exchange:
    def __init__(self, has, peers, q_ref, yh_ref, left_ref, right_ref, send, recv):
        rows, cols = q_ref.shape[1:]
        last = slice(cols - LANES, cols)
        first = slice(0, LANES)
        before, after = slice(HALO, 2 * HALO), slice(0, HALO)
        block, rim = slice(0, rows), slice(rows, rows + 2 * HALO)

        def copy(source, target, slot, peer):
            return pltpu.make_async_remote_copy(
                src_ref=source,
                dst_ref=target,
                send_sem=send.at[slot],
                recv_sem=recv.at[slot],
                device_id=peer,
                device_id_type=MESH,
            )

        self.has = has
        self.sides = left_ref, right_ref
        self.targets = yh_ref.at[:, after], yh_ref.at[:, before], right_ref, left_ref
        self.blocks = (
            copy(q_ref.at[:, rows - HALO : rows], yh_ref.at[:, before], 0, peers[0]),
            copy(q_ref.at[:, 0:HALO], yh_ref.at[:, after], 1, peers[1]),
            copy(q_ref.at[:, :, last], left_ref.at[:, block], 2, peers[2]),
            copy(q_ref.at[:, :, first], right_ref.at[:, block], 3, peers[3]),
        )
        self.rims = (
            copy(yh_ref.at[:, :, last], left_ref.at[:, rim], 4, peers[2]),
            copy(yh_ref.at[:, :, first], right_ref.at[:, rim], 5, peers[3]),
        )

    def clear(self):
        for there, target in zip(self.has, self.targets):

            @pl.when(jnp.logical_not(there))
            def _():
                target[...] = jnp.zeros(target.shape, F32)

    def start(self):
        each(zip(self.has, [copy.start for copy in self.blocks]))

    def forward(self):
        up, down, right, left = self.has
        each([(down, self.blocks[0].wait_recv), (up, self.blocks[1].wait_recv)])
        each([(right, self.rims[0].start), (left, self.rims[1].start)])

    def finish(self):
        up, down, right, left = self.has
        each([(left, self.blocks[2].wait_recv), (right, self.blocks[3].wait_recv)])
        each([(left, self.rims[0].wait_recv), (right, self.rims[1].wait_recv)])
        each(zip(self.has, [copy.wait_send for copy in self.blocks]))
        each([(right, self.rims[0].wait_send), (left, self.rims[1].wait_send)])

    def tile(self, x):
        left_ref, right_ref = self.sides
        lane = lax.broadcasted_iota(jnp.int32, left_ref.shape[1:], 1)
        return jnp.where(lane < LANES // 2, right_ref[x], left_ref[x])


def update_kernel(
    count_y, count_z, part_ref, old_ref, factor_ref, out_ref, shares, half, held,
    send_z, recv_z, send_y, recv_y, send_y2, recv_y2, send_z2, recv_z2
):
    me_y, me_z = lax.axis_index("ha"), lax.axis_index("dev")
    large, rows = half.shape[0], held.shape[1]
    barrier = pltpu.get_barrier_semaphore()
    peers_y = [lax.rem(me_y + d, count_y) for d in range(1, count_y)]
    peers_z = [lax.rem(me_z + d, count_z) for d in range(1, count_z)]
    for axis, peers in (("ha", peers_y), ("dev", peers_z)):
        for peer in peers:
            pl.semaphore_signal(barrier, inc=1, device_id={axis: peer}, device_id_type=MESH)
    pl.semaphore_wait(barrier, count_y + count_z - 2)

    def copy(source, target, send, recv, axis, peer):
        started = pltpu.make_async_remote_copy(
            src_ref=source,
            dst_ref=target,
            send_sem=send,
            recv_sem=recv,
            device_id={axis: peer},
            device_id_type=MESH,
        )
        started.start()
        return started

    def span(index, size):
        return pl.ds(pl.multiple_of(index * size, size), size)

    mine_z = span(me_z, large)
    mine = pl.ds(pl.multiple_of(me_z * large + me_y * rows, rows), rows)
    copies = [
        copy(part_ref.at[span(peer, large)], shares.at[d], send_z.at[d], recv_z.at[d], "dev", peer)
        for d, peer in enumerate(peers_z)
    ]
    total = part_ref[mine_z]
    for d, started in enumerate(copies):
        started.wait_recv()
        total = total + shares[d]
    half[...] = total
    copies += [
        copy(half.at[span(peer, rows)], held.at[d], send_y.at[d], recv_y.at[d], "ha", peer)
        for d, peer in enumerate(peers_y)
    ]
    total = half[span(me_y, rows)]
    for d, started in enumerate(copies[count_z - 1 :]):
        started.wait_recv()
        total = total + held[d]
    out_ref[mine] = old_ref[mine] + factor_ref[mine] * total
    for started in copies:
        started.wait_send()
    copies = [
        copy(out_ref.at[mine], out_ref.at[mine], send_y2.at[d], recv_y2.at[d], "ha", peer)
        for d, peer in enumerate(peers_y)
    ]
    for started in copies:
        started.wait()
    copies = [
        copy(out_ref.at[mine_z], out_ref.at[mine_z], send_z2.at[d], recv_z2.at[d], "dev", peer)
        for d, peer in enumerate(peers_z)
    ]
    for started in copies:
        started.wait()


VMEM = pl.BlockSpec(memory_space=pltpu.VMEM)
SMEM = pl.BlockSpec(memory_space=pltpu.SMEM)
PARAMS = pltpu.CompilerParams(vmem_limit_bytes=60 * 1024 * 1024)


def per_device(brain_image, adjoint_field, velocity_modes):
    planes, rows, cols = brain_image.shape
    count_y = lax.axis_size("ha")
    count_z = lax.axis_size("dev")
    height, depth = rows * count_y, cols * count_z
    modes_x, modes = velocity_modes.shape[1:3]
    tall, wide = rows + 2 * HALO, cols + LANES

    expand_y, expand_z, project_y, project_z = [], [], [], []
    for i in range(count_y):
        positions = np.arange(i * rows - HALO, (i + 1) * rows + HALO)
        high, low = halves(basis(positions, height, modes))
        expand_y.append(np.concatenate([high, high, low], axis=1))
        high, low = high[HALO:-HALO].T, low[HALO:-HALO].T
        project_y.append(np.concatenate([high, high, low], axis=1))
    for i in range(count_z):
        high, low = halves(basis(wrapped(i * cols, cols, wide, depth), depth, modes))
        high, low = high.T, low.T
        table = np.zeros((LANES, wide), ml_dtypes.bfloat16)
        table[: 3 * modes] = np.concatenate([high, low, high], axis=0)
        expand_z.append(table)
        table = np.zeros((3, cols, 2, LANES), ml_dtypes.bfloat16)
        for c in range(3):
            table[c, :, 0, c * modes : (c + 1) * modes] = high.T[:cols]
            table[c, :, 1, c * modes : (c + 1) * modes] = low.T[:cols]
        project_z.append(table.reshape(3 * cols, 2 * LANES))

    by_wide, by_back = jnp.asarray(np.stack(expand_y)), jnp.asarray(np.stack(project_y))
    bz_wide, bz_back = jnp.asarray(np.stack(expand_z)), jnp.asarray(np.stack(project_z))
    bx = jnp.asarray(basis(np.arange(planes), planes, modes_x))
    factor = mode_factor((planes, height, depth), (modes_x, modes, modes))
    factor = np.tile(factor, (1, 1, LANES // modes)).astype(np.float32).reshape(-1, LANES)
    scale = 1.0 / math.sqrt(modes_x * modes * modes)

    def widen(value):
        return jnp.pad(value, ((0, 0), (0, 0), (0, LANES - 3 * modes)))

    plane = pltpu.VMEM((wide // LANES, planes + 2, tall + 2 * HALO, LANES), F32)
    block = jax.ShapeDtypeStruct((planes, rows, cols), F32)
    rims = jax.ShapeDtypeStruct((planes, 2 * HALO, cols), F32)
    sheet = jax.ShapeDtypeStruct((planes, tall, LANES), F32)
    work = [plane, plane] + [pltpu.VMEM((planes, tall, wide), F32)] * 7
    adjoint_transport = pl.pallas_call(
        functools.partial(adjoint_kernel, planes, modes_x, modes, count_y, count_z),
        out_shape=(block, rims, sheet),
        in_specs=[VMEM, SMEM, VMEM, VMEM, VMEM, VMEM],
        out_specs=(VMEM, VMEM, VMEM),
        scratch_shapes=[pltpu.VMEM(rims.shape, F32)]
        + [pltpu.VMEM(sheet.shape, F32)] * 4
        + [pltpu.SemaphoreType.DMA((6,))] * 4
        + work,
        compiler_params=pltpu.CompilerParams(
            vmem_limit_bytes=60 * 1024 * 1024, collective_id=1, has_side_effects=True
        ),
        name="adjoint_transport",
    )
    image_transport = pl.pallas_call(
        functools.partial(image_kernel, planes, modes_x, modes),
        out_shape=(block, jax.ShapeDtypeStruct(velocity_modes.shape, F32)),
        in_specs=[VMEM, SMEM, VMEM, VMEM, VMEM, VMEM, VMEM],
        out_specs=(VMEM, VMEM),
        scratch_shapes=work,
        compiler_params=PARAMS,
        name="image_transport",
    )
    project = pl.pallas_call(
        functools.partial(project_kernel, planes, modes_x),
        out_shape=jax.ShapeDtypeStruct((modes_x, modes, LANES), F32),
        in_specs=[VMEM, VMEM, VMEM, VMEM, SMEM, VMEM, VMEM],
        out_specs=VMEM,
        scratch_shapes=[
            plane,
            pltpu.VMEM((planes * 2 * rows, 3 * cols), BF16),
            pltpu.VMEM((planes, rows, LANES), F32),
        ],
        compiler_params=PARAMS,
        name="project",
    )

    entries = modes_x * modes
    update = pl.pallas_call(
        functools.partial(update_kernel, count_y, count_z),
        out_shape=jax.ShapeDtypeStruct((entries, LANES), F32),
        in_specs=[VMEM, VMEM, VMEM],
        out_specs=VMEM,
        scratch_shapes=[
            pltpu.VMEM((count_z, entries // count_z, LANES), F32),
            pltpu.VMEM((entries // count_z, LANES), F32),
            pltpu.VMEM((count_y, entries // count_z // count_y, LANES), F32),
        ]
        + [pltpu.SemaphoreType.DMA((n,)) for n in (count_z,) * 2 + (count_y,) * 4 + (count_z,) * 2],
        compiler_params=pltpu.CompilerParams(collective_id=0, has_side_effects=True),
        name="update",
    )

    old = widen(velocity_modes.transpose(1, 2, 0, 3).reshape(modes_x, modes, 3 * modes))
    adjoint_end, *image_halo = adjoint_transport(
        old, bx * -scale, by_wide, bz_wide, adjoint_field, brain_image
    )
    partial = project(adjoint_end, brain_image, *image_halo, bx, by_back, bz_back)
    updated = update(partial.reshape(entries, LANES), old.reshape(entries, LANES), factor)
    image_end, velocity_next = image_transport(
        updated.reshape(modes_x, modes, LANES),
        bx * scale,
        by_wide,
        bz_wide,
        brain_image,
        *image_halo,
    )
    return (adjoint_end, image_end, velocity_next)


def solution(mesh):
    placed = (P("subj", "ha", "dev"), P("subj", "ha", "dev"), P("subj", None, None, None))
    return jax.shard_map(
        per_device,
        mesh=mesh,
        in_specs=placed,
        out_specs=placed,
        check_vma=False,
    )
```

```python
import functools
import math

import jax
import jax.numpy as jnp
import ml_dtypes
import numpy as np
from jax import lax
from jax.experimental import pallas as pl
from jax.experimental.pallas import tpu as pltpu
from jax.sharding import PartitionSpec as P

STEPS = 4
HALO = 2 * STEPS
STEP_SIZE = 4.0
STIFFNESS = 2.0
LANES = 128
F32 = jnp.float32
BF16 = jnp.bfloat16


def wavenumbers(modes):
    column = np.arange(modes)
    return np.where(column <= modes // 2, column, column - modes // 2)


def basis(positions, length, modes):
    phase = positions[:, None] * wavenumbers(modes)[None, :] % length
    angles = phase * (2.0 * math.pi / length)
    cosine = np.arange(modes)[None, :] <= modes // 2
    table = np.where(cosine, np.cos(angles), np.sin(angles))
    inside = (positions >= 0) & (positions < length)
    return np.where(inside[:, None], table, 0.0).astype(np.float32)


def halves(table):
    high = table.astype(ml_dtypes.bfloat16)
    low = (table - high.astype(np.float32)).astype(ml_dtypes.bfloat16)
    return high, low


def wrapped(start, rows, total, length):
    gap = np.full(total - rows - 2 * HALO, -1)
    after = np.arange(start + rows, start + rows + HALO)
    before = np.arange(start - HALO, start)
    return np.concatenate([np.arange(start, start + rows), after, gap, before])


def mode_factor(lengths, modes):
    eigen, weight = [], []
    for length, count in zip(lengths, modes):
        eigen.append(2.0 - 2.0 * np.cos(wavenumbers(count) * (2.0 * math.pi / length)))
        weight.append(np.where(np.arange(count) == 0, length, length / 2.0))
    value = eigen[0][:, None, None] + eigen[1][None, :, None] + eigen[2][None, None, :]
    norm = weight[0][:, None, None] * weight[1][None, :, None] * weight[2][None, None, :]
    return STEP_SIZE * math.sqrt(math.prod(modes)) / (norm * (1.0 + STIFFNESS * value) ** 2)


def split(value):
    high = value.astype(BF16)
    return high, (value - high.astype(F32)).astype(BF16)


def expand_kernel(planes, modes_x, modes, v_ref, bx_ref, by_ref, bz_ref, coefs):
    height, depth = coefs[0].shape[1:]
    by, bz = by_ref[lax.axis_index("ha")], bz_ref.at[lax.axis_index("dev")]
    group = lax.broadcasted_iota(jnp.int32, (height, LANES), 1) // modes

    def body(x, carry):
        weighted = bx_ref[x, 0] * v_ref[0]
        for a in range(1, modes_x):
            weighted = weighted + bx_ref[x, a] * v_ref[a]
        high, low = split(weighted)
        rows = jnp.concatenate([high, low, high], axis=0)
        mixed = jnp.dot(by, rows, preferred_element_type=F32)
        top = mixed.astype(BF16).astype(F32)
        rest = mixed - top
        total = jnp.ones((height, depth), F32)
        for c in range(3):
            first = pltpu.roll(top, (-c * modes) % LANES, 1) if c else top
            second = pltpu.roll(top, ((1 - c) * modes) % LANES, 1) if c != 1 else top
            third = pltpu.roll(rest, ((2 - c) * modes) % LANES, 1) if c != 2 else rest
            left = jnp.where(group == 0, first, jnp.where(group == 1, second, third))
            speed = jnp.dot(left.astype(BF16), bz[...], preferred_element_type=F32)
            plus = jnp.maximum(speed, 0.0)
            minus = jnp.maximum(-speed, 0.0)
            coefs[1 + 2 * c][x] = plus
            coefs[2 + 2 * c][x] = minus
            total = total - (plus + minus)
        coefs[0][x] = total
        return carry

    lax.fori_loop(0, planes, body, 0, unroll=4)


def gather_field(q_ref, yh_ref, tile, field):
    tiles, height = field.shape[0], field.shape[2]
    planes, rows, depth = q_ref.shape
    edge = jnp.zeros((height, LANES), F32)
    spare = jnp.zeros((HALO, LANES), F32)
    block = slice(2 * HALO, 2 * HALO + rows)
    after = slice(2 * HALO + rows, 3 * HALO + rows)
    before = slice(HALO, 2 * HALO)
    for t in range(tiles):
        field[t, 0] = edge
        field[t, planes + 1] = edge

    def body(x, carry):
        side = tile(x)
        for t in range(tiles):
            lanes = slice(t * LANES, (t + 1) * LANES)
            field[t, x + 1, 0:HALO] = spare
            field[t, x + 1, height - HALO : height] = spare
            last = t == tiles - 1
            field[t, x + 1, block] = side[0:rows] if last else q_ref[x, :, lanes]
            field[t, x + 1, after] = (
                side[rows : rows + HALO] if last else yh_ref[x, 0:HALO, lanes]
            )
            field[t, x + 1, before] = (
                side[rows + HALO :] if last else yh_ref[x, HALO : 2 * HALO, lanes]
            )
        return carry

    lax.fori_loop(0, planes, body, 0)


def clear_edges(middle):
    tiles, planes, height = middle.shape[:3]
    edge = jnp.zeros((height, LANES), F32)
    spare = jnp.zeros((HALO, LANES), F32)
    for t in range(tiles):
        middle[t, 0] = edge
        middle[t, planes - 1] = edge

    def body(x, carry):
        for t in range(tiles):
            middle[t, x, 0:HALO] = spare
            middle[t, x, height - HALO : height] = spare
        return carry

    lax.fori_loop(0, planes, body, 0)


def stencil(src, start, group, coefs, strips, tiles):
    lane = lax.broadcasted_iota(jnp.int32, (8, LANES), 1)
    count = src.shape[0]
    for t in strips:
        row = HALO + 8 * t
        planes = [
            [src[k, start + i, row : row + 8] for k in range(count)] for i in range(group + 2)
        ]
        for i in range(group):
            x = start + i
            here = planes[i + 1]
            ahead = [pltpu.roll(value, 1, 1) for value in here]
            back = [pltpu.roll(value, LANES - 1, 1) for value in here]
            for k in range(tiles):

                def coef(index):
                    return coefs[index][x, 8 * t : 8 * t + 8, k * LANES : (k + 1) * LANES]

                total = coef(0) * here[k]
                total = total + (coef(1) * planes[i][k] + coef(2) * planes[i + 2][k])
                total = total + (
                    coef(3) * src[k, x + 1, row - 1 : row + 7]
                    + coef(4) * src[k, x + 1, row + 1 : row + 9]
                )
                left = jnp.where(lane == 0, ahead[k - 1], ahead[k])
                right = jnp.where(lane == LANES - 1, back[(k + 1) % count], back[k])
                yield x, t, k, total + (coef(5) * left + coef(6) * right)


def transport(planes, q_ref, out_ref, field, middle, coefs, between):
    tiles = field.shape[0]
    rows, depth = q_ref.shape[1:]
    strips = (rows + 2 * HALO) // 8
    scale = 0.5**STEPS

    group = math.gcd(planes, 4)

    def first(i, carry):
        for x, t, k, value in stencil(field, group * i, group, coefs, range(strips), tiles):
            middle[k, x + 1, HALO + 8 * t : HALO + 8 * t + 8] = value
        return carry

    def second(i, carry):
        for x, t, k, value in stencil(middle, group * i, group, coefs, range(strips), tiles):
            part = slice(HALO + 8 * t, HALO + 8 * t + 8)
            field[k, x + 1, part] = field[k, x + 1, part] + value
        return carry

    def last(i, carry):
        inner = range(HALO // 8, strips - HALO // 8)
        for x, t, k, value in stencil(middle, group * i, group, coefs, inner, depth // LANES):
            part = slice(HALO + 8 * t, HALO + 8 * t + 8)
            lanes = slice(k * LANES, (k + 1) * LANES)
            row = 8 * t - HALO
            out_ref[x, row : row + 8, lanes] = scale * (field[k, x + 1, part] + value)
        return carry

    def step(i, carry):
        lax.fori_loop(0, planes // group, first, 0, unroll=2)
        lax.fori_loop(0, planes // group, second, 0, unroll=2)
        return carry

    lax.fori_loop(0, STEPS - 1, step, 0)
    between()
    lax.fori_loop(0, planes // group, first, 0, unroll=2)
    lax.fori_loop(0, planes // group, last, 0, unroll=2)


def adjoint_kernel(
    planes, modes_x, modes, count_y, count_z, v_ref, bx_ref, by_ref, bz_ref, q_ref, image_ref,
    out_ref, image_yh, image_zt, old_ref, yh_ref, left, right, image_left, image_right,
    send, recv, image_send, image_recv, field, middle, *coefs
):
    has, peers = neighbours(count_y, count_z)
    mine = Exchange(has, peers, q_ref, yh_ref, left, right, send, recv)
    image = Exchange(
        has, peers, image_ref, image_yh, image_left, image_right, image_send, image_recv
    )
    mine.clear()
    image.clear()
    greet(has, peers)
    mine.start()
    clear_edges(middle)
    blank = jnp.zeros((modes, LANES - 3 * modes), F32)
    for a in range(modes_x):
        old_ref[a] = jnp.concatenate([v_ref[c, a] for c in range(3)] + [blank], axis=1)
    expand_kernel(planes, modes_x, modes, old_ref, bx_ref, by_ref, bz_ref, coefs)
    mine.forward()
    image.start()
    mine.finish()
    gather_field(q_ref, yh_ref, mine.tile, field)
    transport(planes, q_ref, out_ref, field, middle, coefs, image.forward)
    image.finish()

    def merge(x, carry):
        image_zt[x] = image.tile(x)
        return carry

    lax.fori_loop(0, planes, merge, 0)


def image_kernel(
    planes, modes_x, modes, v_ref, bx_ref, by_ref, bz_ref, q_ref, yh_ref, zt_ref,
    out_ref, next_ref, field, middle, *coefs
):
    for c in range(3):
        for a in range(modes_x):
            next_ref[c, a] = v_ref[a][:, c * modes : (c + 1) * modes]
    clear_edges(middle)
    gather_field(q_ref, yh_ref, lambda x: zt_ref[x], field)
    expand_kernel(planes, modes_x, modes, v_ref, bx_ref, by_ref, bz_ref, coefs)
    transport(planes, q_ref, out_ref, field, middle, coefs, lambda: None)


def project_kernel(
    planes, modes_x, adj_ref, q_ref, yh_ref, zt_ref, bx_ref, by_ref, bz_ref, out_ref, field, forcing, inner
):
    rows, depth = q_ref.shape[1:]
    tiles = field.shape[0]
    gather_field(q_ref, yh_ref, lambda x: zt_ref[x], field)
    by, bz = by_ref[lax.axis_index("ha")], bz_ref.at[lax.axis_index("dev")]
    start = 2 * HALO

    def body(x, carry):
        half = 0.5 * adj_ref[x]

        def take(plane, offset):
            part = slice(start + offset, start + offset + rows)
            parts = [field[k, plane, part] for k in range(depth // LANES)]
            return jnp.concatenate(parts, axis=1)

        row = jnp.concatenate([field[k, x + 1, start : start + rows] for k in range(tiles)], axis=1)
        width = tiles * LANES
        slopes = (
            take(x + 2, 0) - take(x, 0),
            take(x + 1, 1) - take(x + 1, -1),
            (pltpu.roll(row, width - 1, 1) - pltpu.roll(row, 1, 1))[:, 0:depth],
        )
        for c in range(3):
            high, low = split(half * slopes[c])
            columns = slice(c * depth, (c + 1) * depth)
            forcing[pl.ds(x * 2 * rows, rows), columns] = high
            forcing[pl.ds(x * 2 * rows + rows, rows), columns] = low
        return carry

    lax.fori_loop(0, planes, body, 0, unroll=2)
    chunk = 8

    def multiply(i, carry):
        start = i * (chunk * 2 * rows)
        wide = jnp.dot(
            forcing[pl.ds(start, chunk * 2 * rows), :], bz[...], preferred_element_type=F32
        )
        wide = wide[:, 0:LANES] + wide[:, LANES : 2 * LANES]
        wide = wide.reshape(chunk, 2 * rows, LANES)
        inner[pl.ds(i * chunk, chunk)] = wide[:, 0:rows] + wide[:, rows : 2 * rows]
        return carry

    lax.fori_loop(0, planes // chunk, multiply, 0)

    def finish(a, carry):
        total = bx_ref[0, a] * inner[0]
        for x in range(1, planes):
            total = total + bx_ref[x, a] * inner[x]
        high, low = split(total)
        stacked = jnp.concatenate([high, low, high], axis=0)
        out_ref[a] = jnp.dot(by, stacked, preferred_element_type=F32)
        return carry

    lax.fori_loop(0, modes_x, finish, 0, unroll=2)


MESH = pl.DeviceIdType.MESH


def neighbours(count_y, count_z):
    me_y, me_z = lax.axis_index("ha"), lax.axis_index("dev")
    has = (me_y < count_y - 1, me_y > 0, me_z < count_z - 1, me_z > 0)
    peers = ({"ha": me_y + 1}, {"ha": me_y - 1}, {"dev": me_z + 1}, {"dev": me_z - 1})
    return has, peers


def each(pairs):
    for there, action in pairs:

        @pl.when(there)
        def _():
            action()


def greet(has, peers):
    barrier = pltpu.get_barrier_semaphore()
    for there, peer in zip(has, peers):

        @pl.when(there)
        def _():
            pl.semaphore_signal(barrier, inc=1, device_id=peer, device_id_type=MESH)

    pl.semaphore_wait(barrier, sum(jnp.where(there, 1, 0) for there in has))


class Exchange:
    def __init__(self, has, peers, q_ref, yh_ref, left_ref, right_ref, send, recv):
        rows, cols = q_ref.shape[1:]
        last = slice(cols - LANES, cols)
        first = slice(0, LANES)
        before, after = slice(HALO, 2 * HALO), slice(0, HALO)
        block, rim = slice(0, rows), slice(rows, rows + 2 * HALO)

        def copy(source, target, slot, peer):
            return pltpu.make_async_remote_copy(
                src_ref=source,
                dst_ref=target,
                send_sem=send.at[slot],
                recv_sem=recv.at[slot],
                device_id=peer,
                device_id_type=MESH,
            )

        self.has = has
        self.sides = left_ref, right_ref
        self.targets = yh_ref.at[:, after], yh_ref.at[:, before], right_ref, left_ref
        self.blocks = (
            copy(q_ref.at[:, rows - HALO : rows], yh_ref.at[:, before], 0, peers[0]),
            copy(q_ref.at[:, 0:HALO], yh_ref.at[:, after], 1, peers[1]),
            copy(q_ref.at[:, :, last], left_ref.at[:, block], 2, peers[2]),
            copy(q_ref.at[:, :, first], right_ref.at[:, block], 3, peers[3]),
        )
        self.rims = (
            copy(yh_ref.at[:, :, last], left_ref.at[:, rim], 4, peers[2]),
            copy(yh_ref.at[:, :, first], right_ref.at[:, rim], 5, peers[3]),
        )

    def clear(self):
        for there, target in zip(self.has, self.targets):

            @pl.when(jnp.logical_not(there))
            def _():
                target[...] = jnp.zeros(target.shape, F32)

    def start(self):
        each(zip(self.has, [copy.start for copy in self.blocks]))

    def forward(self):
        up, down, right, left = self.has
        each([(down, self.blocks[0].wait_recv), (up, self.blocks[1].wait_recv)])
        each([(right, self.rims[0].start), (left, self.rims[1].start)])

    def finish(self):
        up, down, right, left = self.has
        each([(left, self.blocks[2].wait_recv), (right, self.blocks[3].wait_recv)])
        each([(left, self.rims[0].wait_recv), (right, self.rims[1].wait_recv)])
        each(zip(self.has, [copy.wait_send for copy in self.blocks]))
        each([(right, self.rims[0].wait_send), (left, self.rims[1].wait_send)])

    def tile(self, x):
        left_ref, right_ref = self.sides
        lane = lax.broadcasted_iota(jnp.int32, left_ref.shape[1:], 1)
        return jnp.where(lane < LANES // 2, right_ref[x], left_ref[x])


def update_kernel(
    count_y, count_z, part_ref, old_ref, factor_ref, out_ref, shares, half, held,
    send_z, recv_z, send_y, recv_y, send_y2, recv_y2, send_z2, recv_z2
):
    me_y, me_z = lax.axis_index("ha"), lax.axis_index("dev")
    large, rows = half.shape[0], held.shape[1]
    barrier = pltpu.get_barrier_semaphore()
    peers_y = [lax.rem(me_y + d, count_y) for d in range(1, count_y)]
    peers_z = [lax.rem(me_z + d, count_z) for d in range(1, count_z)]
    for axis, peers in (("ha", peers_y), ("dev", peers_z)):
        for peer in peers:
            pl.semaphore_signal(barrier, inc=1, device_id={axis: peer}, device_id_type=MESH)
    pl.semaphore_wait(barrier, count_y + count_z - 2)

    def copy(source, target, send, recv, axis, peer):
        started = pltpu.make_async_remote_copy(
            src_ref=source,
            dst_ref=target,
            send_sem=send,
            recv_sem=recv,
            device_id={axis: peer},
            device_id_type=MESH,
        )
        started.start()
        return started

    def span(index, size):
        return pl.ds(pl.multiple_of(index * size, size), size)

    mine_z = span(me_z, large)
    mine = pl.ds(pl.multiple_of(me_z * large + me_y * rows, rows), rows)
    copies = [
        copy(part_ref.at[span(peer, large)], shares.at[d], send_z.at[d], recv_z.at[d], "dev", peer)
        for d, peer in enumerate(peers_z)
    ]
    total = part_ref[mine_z]
    for d, started in enumerate(copies):
        started.wait_recv()
        total = total + shares[d]
    half[...] = total
    copies += [
        copy(half.at[span(peer, rows)], held.at[d], send_y.at[d], recv_y.at[d], "ha", peer)
        for d, peer in enumerate(peers_y)
    ]
    total = half[span(me_y, rows)]
    for d, started in enumerate(copies[count_z - 1 :]):
        started.wait_recv()
        total = total + held[d]
    out_ref[mine] = old_ref[mine] + factor_ref[mine] * total
    for started in copies:
        started.wait_send()
    copies = [
        copy(out_ref.at[mine], out_ref.at[mine], send_y2.at[d], recv_y2.at[d], "ha", peer)
        for d, peer in enumerate(peers_y)
    ]
    for started in copies:
        started.wait()
    copies = [
        copy(out_ref.at[mine_z], out_ref.at[mine_z], send_z2.at[d], recv_z2.at[d], "dev", peer)
        for d, peer in enumerate(peers_z)
    ]
    for started in copies:
        started.wait()


VMEM = pl.BlockSpec(memory_space=pltpu.VMEM)
SMEM = pl.BlockSpec(memory_space=pltpu.SMEM)
PARAMS = pltpu.CompilerParams(vmem_limit_bytes=60 * 1024 * 1024)


def per_device(brain_image, adjoint_field, velocity_modes):
    planes, rows, cols = brain_image.shape
    count_y = lax.axis_size("ha")
    count_z = lax.axis_size("dev")
    height, depth = rows * count_y, cols * count_z
    modes_x, modes = velocity_modes.shape[1:3]
    tall, wide = rows + 2 * HALO, cols + LANES

    expand_y, expand_z, project_y, project_z = [], [], [], []
    for i in range(count_y):
        positions = np.arange(i * rows - HALO, (i + 1) * rows + HALO)
        high, low = halves(basis(positions, height, modes))
        expand_y.append(np.concatenate([high, high, low], axis=1))
        high, low = high[HALO:-HALO].T, low[HALO:-HALO].T
        project_y.append(np.concatenate([high, high, low], axis=1))
    for i in range(count_z):
        high, low = halves(basis(wrapped(i * cols, cols, wide, depth), depth, modes))
        high, low = high.T, low.T
        table = np.zeros((LANES, wide), ml_dtypes.bfloat16)
        table[: 3 * modes] = np.concatenate([high, low, high], axis=0)
        expand_z.append(table)
        table = np.zeros((3, cols, 2, LANES), ml_dtypes.bfloat16)
        for c in range(3):
            table[c, :, 0, c * modes : (c + 1) * modes] = high.T[:cols]
            table[c, :, 1, c * modes : (c + 1) * modes] = low.T[:cols]
        project_z.append(table.reshape(3 * cols, 2 * LANES))

    by_wide, by_back = jnp.asarray(np.stack(expand_y)), jnp.asarray(np.stack(project_y))
    bz_wide, bz_back = jnp.asarray(np.stack(expand_z)), jnp.asarray(np.stack(project_z))
    bx = jnp.asarray(basis(np.arange(planes), planes, modes_x))
    factor = mode_factor((planes, height, depth), (modes_x, modes, modes))
    factor = np.tile(factor, (1, 1, LANES // modes)).astype(np.float32).reshape(-1, LANES)
    scale = 1.0 / math.sqrt(modes_x * modes * modes)

    plane = pltpu.VMEM((wide // LANES, planes + 2, tall + 2 * HALO, LANES), F32)
    block = jax.ShapeDtypeStruct((planes, rows, cols), F32)
    rims = jax.ShapeDtypeStruct((planes, 2 * HALO, cols), F32)
    sheet = jax.ShapeDtypeStruct((planes, tall, LANES), F32)
    work = [plane, plane] + [pltpu.VMEM((planes, tall, wide), F32)] * 7
    adjoint_transport = pl.pallas_call(
        functools.partial(adjoint_kernel, planes, modes_x, modes, count_y, count_z),
        out_shape=(
            block, rims, sheet, jax.ShapeDtypeStruct((modes_x, modes, LANES), F32)
        ),
        in_specs=[VMEM, SMEM, VMEM, VMEM, VMEM, VMEM],
        out_specs=(VMEM,) * 4,
        scratch_shapes=[pltpu.VMEM(rims.shape, F32)]
        + [pltpu.VMEM(sheet.shape, F32)] * 4
        + [pltpu.SemaphoreType.DMA((6,))] * 4
        + work,
        compiler_params=pltpu.CompilerParams(
            vmem_limit_bytes=60 * 1024 * 1024, collective_id=1, has_side_effects=True
        ),
        name="adjoint_transport",
    )
    image_transport = pl.pallas_call(
        functools.partial(image_kernel, planes, modes_x, modes),
        out_shape=(block, jax.ShapeDtypeStruct(velocity_modes.shape, F32)),
        in_specs=[VMEM, SMEM, VMEM, VMEM, VMEM, VMEM, VMEM],
        out_specs=(VMEM, VMEM),
        scratch_shapes=work,
        compiler_params=PARAMS,
        name="image_transport",
    )
    project = pl.pallas_call(
        functools.partial(project_kernel, planes, modes_x),
        out_shape=jax.ShapeDtypeStruct((modes_x, modes, LANES), F32),
        in_specs=[VMEM, VMEM, VMEM, VMEM, SMEM, VMEM, VMEM],
        out_specs=VMEM,
        scratch_shapes=[
            plane,
            pltpu.VMEM((planes * 2 * rows, 3 * cols), BF16),
            pltpu.VMEM((planes, rows, LANES), F32),
        ],
        compiler_params=PARAMS,
        name="project",
    )

    entries = modes_x * modes
    update = pl.pallas_call(
        functools.partial(update_kernel, count_y, count_z),
        out_shape=jax.ShapeDtypeStruct((entries, LANES), F32),
        in_specs=[VMEM, VMEM, VMEM],
        out_specs=VMEM,
        scratch_shapes=[
            pltpu.VMEM((count_z, entries // count_z, LANES), F32),
            pltpu.VMEM((entries // count_z, LANES), F32),
            pltpu.VMEM((count_y, entries // count_z // count_y, LANES), F32),
        ]
        + [pltpu.SemaphoreType.DMA((n,)) for n in (count_z,) * 2 + (count_y,) * 4 + (count_z,) * 2],
        compiler_params=pltpu.CompilerParams(collective_id=0, has_side_effects=True),
        name="update",
    )

    adjoint_end, *image_halo, old = adjoint_transport(
        velocity_modes, bx * -scale, by_wide, bz_wide, adjoint_field, brain_image
    )
    partial = project(adjoint_end, brain_image, *image_halo, bx, by_back, bz_back)
    updated = update(partial.reshape(entries, LANES), old.reshape(entries, LANES), factor)
    image_end, velocity_next = image_transport(
        updated.reshape(modes_x, modes, LANES),
        bx * scale,
        by_wide,
        bz_wide,
        brain_image,
        *image_halo,
    )
    return (adjoint_end, image_end, velocity_next)


def solution(mesh):
    placed = (P("subj", "ha", "dev"), P("subj", "ha", "dev"), P("subj", None, None, None))
    return jax.shard_map(
        per_device,
        mesh=mesh,
        in_specs=placed,
        out_specs=placed,
        check_vma=False,
    )
```
